32 devices in a mesh: groups: 2 (over x), ctx: 16 (over z, y, core).
Axes of the slice: x: 2, y: 2, z: 4, core: 2. Of those that a mesh axis runs over, the one named last changes fastest.
Arguments:
- keys: bfloat16 [16384, 128], P(('groups', 'ctx')), parts along dimension 0, may hold values from -6 to 6
- queries: bfloat16 [8192, 1024], P(('groups', 'ctx')), parts along dimension 0, may hold values from -240 to 240
- teacher_map: bfloat16 [8192, 512], P(('groups', 'ctx')), parts along dimension 0, may hold values from 0.0099487305 to 1
- slab_index: int32 [32], P(('groups', 'ctx')), parts along dimension 0, may hold values from 0 to 31
- pos_gain: float32 [32, 128], replicated, may hold values from 0.1 to 1.9
- w_comp: bfloat16 [128, 128], replicated, may hold values from -0.09375 to 0.09375
Outputs:
- loss: float32 [2], P('groups'), parts along dimension 0
- grad_queries: bfloat16 [8192, 1024], P(('groups', 'ctx')), parts along dimension 0
- grad_keys: bfloat16 [16384, 128], P(('groups', 'ctx')), parts along dimension 0
- grad_comp: float32 [256, 128], P('groups'), parts along dimension 0
- grad_gain: float32 [64, 128], P('groups'), parts along dimension 0
The draws below stay inside these ranges and needn't reach their ends.
There are 2 independent parts, one for each index of `groups`. The reference program is written for one: setup_inputs(seed, part) draws one part's arguments, and reference() takes and returns one part's arrays. A program takes and returns all parts, laid end to end along the dimension named above; an argument that names none is the same for every part. Nothing has to cross between parts.
All inputs are finite; a program needn't handle non-finite values.
Results may differ from the reference program's by a relative error of at most 0.009.
The reference program's roundings to bfloat16 on the way count: a program that leaves them out, or rounds other values in their place, can miss the bound.
Values may be sent and summed in bfloat16 or wider, within the bound.
A program may use at most 64 MiB of HBM per device.

```python
import math
import jax
import jax.numpy as jnp
from jax import lax

DH = 128
HEADS = 8
KERNEL = 32
STRIDE = 16
QDEV = 256
SEQ = 8192
NBLK = 512
NQ = 4096
N_CTX = 16


def draw_queries(key, part):
    first = jax.random.fold_in(key, 11)
    values = jax.random.truncated_normal(first, -6.0, 6.0, (NQ, HEADS * DH), jnp.float32)
    return values.astype(jnp.bfloat16)


def place_ends(entries, stream_key, low, high):
    shape = entries.shape
    index_at = [jax.random.randint(jax.random.fold_in(stream_key, axis), (), 0, shape[axis]) for axis in range(len(shape))]
    entries = entries.at[tuple(index_at)].set(low)
    longest = shape.index(max(shape))
    index_at[longest] = (index_at[longest] + 1) % shape[longest]
    return entries.at[tuple(index_at)].set(high)


def levels(stream_key, shape, cuts, low, top_value):
    gain = 1.0
    for position, parts in cuts:
        steps = jax.random.uniform(jax.random.fold_in(jax.random.fold_in(stream_key, 6), position), (parts,), jnp.float32, low / len(cuts), top_value / len(cuts))
        gain = gain * jnp.repeat(jnp.exp(steps), shape[position] // parts).reshape((-1,) + (1,) * (len(shape) - 1 - position))
    return gain


def normal_values(own_key, extent, deviation, most, pieces=(), kind=jnp.bfloat16):
    result = jax.random.normal(own_key, extent, jnp.float32) * deviation
    if len(pieces) > 0:
        result = levels(own_key, extent, pieces, -0.22, 0.18) * result
    return jnp.clip(result, min=-most, max=most).astype(kind)


def setup_inputs(seed: int = 0, part: int = 0) -> dict:
    splits = jax.random.split(jax.random.key(seed), 7)
    part_splits = jax.random.split(jax.random.fold_in(splits[6], part), 7)
    return {
        "keys": normal_values(part_splits[0], (SEQ, DH), 1.0, 6.0, ((0, 16),)),
        "queries": draw_queries(jax.random.fold_in(jax.random.fold_in(splits[6], part), 71), part),
        "teacher_map": jnp.clip(jnp.exp(math.log(1.0) - 4.61031033 * jax.random.uniform(part_splits[2], (NQ, NBLK), jnp.float32) ** levels(part_splits[2], (NQ, NBLK), ((0, 16),), -0.2, 0.2)), 0.0099487305, 1.0).astype(jnp.bfloat16),
        "slab_index": place_ends(jax.random.randint(part_splits[3], (N_CTX,), 0, SEQ // QDEV), jax.random.fold_in(part_splits[3], 1), 0, (SEQ // QDEV) - 1).astype(jnp.int32),
        "pos_gain": jnp.clip(1.0 + 0.18 * jax.random.normal(splits[4], (KERNEL, DH), jnp.float32), 0.1, 1.9),
        "w_comp": normal_values(splits[5], (DH, DH), (KERNEL * DH) ** -0.5, 0.09375),
    }


big_negative = -1.0e30
loss_scale = 256.0


def pool_keys(keys, pos_gain):
    padded = jnp.concatenate([keys, jnp.zeros((STRIDE, DH), keys.dtype)], axis=0)
    lower = padded[:SEQ].reshape(NBLK, STRIDE, DH).astype(jnp.float32)
    upper = padded[STRIDE:].reshape(NBLK, STRIDE, DH).astype(jnp.float32)
    pooled = jnp.sum(lower * pos_gain[:STRIDE], axis=1) + jnp.sum(upper * pos_gain[STRIDE:], axis=1)
    return lower, upper, pooled.astype(jnp.bfloat16)


def slab_terms(query_rows, teacher_rows, places, comp):
    inv = DH ** -0.5
    count = query_rows.shape[0]
    heads_f = query_rows.reshape(count, HEADS, DH).astype(jnp.float32)
    comp_f = comp.astype(jnp.float32)
    scores = jnp.einsum("thd,jd->htj", heads_f, comp_f) * inv
    column = jnp.arange(NBLK, dtype=jnp.int32)
    visible = (STRIDE * column + KERNEL - 1)[None, :] <= places[:, None]
    masked = jnp.where(visible[None], scores, big_negative)
    top = jnp.max(masked, axis=2, keepdims=True)
    expo = jnp.where(visible[None], jnp.exp(masked - top), 0.0)
    total = jnp.sum(expo, axis=2, keepdims=True)
    lse = jnp.where(total > 0, top + jnp.log(jnp.where(total > 0, total, 1.0)), 0.0)
    shifted = jnp.where(visible[None], scores - lse, big_negative)
    head_top = jnp.max(shifted, axis=0)
    logm = head_top + jnp.log(jnp.sum(jnp.exp(shifted - head_top), axis=0)) - jnp.log(jnp.float32(HEADS))
    logm = jnp.where(visible, logm, 0.0)
    prob = jnp.where(visible[None], jnp.exp(shifted), 0.0)
    ratio = jnp.where(visible[None], jnp.exp(shifted - logm[None]), 0.0) / HEADS
    teach = teacher_rows.astype(jnp.float32)
    teach_total = jnp.sum(jnp.where(visible, teach, 0.0), axis=1, keepdims=True)
    safe_total = jnp.where(teach_total > 0, teach_total, 1.0)
    tprob = jnp.where(visible, teach / safe_total, 0.0)
    logt = jnp.where(visible, jnp.log(teach) - jnp.log(safe_total), 0.0)
    kl_sum = jnp.sum(tprob * (logt - logm))
    cvec = jnp.sum(tprob[None] * ratio, axis=2)
    grad = (loss_scale * (prob * cvec[..., None] - tprob[None] * ratio)).astype(jnp.bfloat16)
    grad_f = grad.astype(jnp.float32)
    grad_q = jnp.einsum("htj,jd->thd", grad_f, comp_f) * inv
    grad_c = jnp.einsum("htj,thd->jd", grad_f, heads_f) * inv
    return kl_sum, grad_q.reshape(count, HEADS * DH).astype(jnp.bfloat16), grad_c


def reference(keys, queries, teacher_map, slab_index, pos_gain, w_comp):
    lower, upper, pooled = pool_keys(keys, pos_gain)
    comp = jnp.dot(pooled, w_comp, preferred_element_type=jnp.float32).astype(jnp.bfloat16)
    places = slab_index[:, None] * QDEV + jnp.arange(QDEV, dtype=jnp.int32)[None, :]

    def step(carry, items):
        q_rows, t_rows, p_rows = items
        kl_sum, grad_q, grad_c = slab_terms(q_rows, t_rows, p_rows, comp)
        return (carry[0] + kl_sum, carry[1] + grad_c), grad_q

    start = (jnp.zeros((), jnp.float32), jnp.zeros((NBLK, DH), jnp.float32))
    items = (queries.reshape(N_CTX, QDEV, HEADS * DH), teacher_map.reshape(N_CTX, QDEV, NBLK), places)
    (kl_total, grad_comp_keys), grad_rows = lax.scan(step, start, items)
    loss = (kl_total / NQ).reshape(1)
    grad_queries = grad_rows.reshape(NQ, HEADS * DH)
    highest = lax.Precision.HIGHEST
    grad_pooled = jnp.dot(grad_comp_keys, w_comp.astype(jnp.float32).T, precision=highest)
    grad_comp = jnp.dot(pooled.astype(jnp.float32).T, grad_comp_keys, precision=highest)
    gain_low = jnp.einsum("jd,jpd->pd", grad_pooled, lower, precision=highest)
    gain_high = jnp.einsum("jd,jpd->pd", grad_pooled, upper, precision=highest)
    grad_gain = jnp.concatenate([gain_low, gain_high], axis=0)
    low_part = (grad_pooled[:, None, :] * pos_gain[:STRIDE]).reshape(SEQ, DH)
    high_part = (grad_pooled[:, None, :] * pos_gain[STRIDE:]).reshape(SEQ, DH)
    shifted_high = jnp.concatenate([jnp.zeros((STRIDE, DH), jnp.float32), high_part[:-STRIDE]], axis=0)
    grad_keys = (low_part + shifted_high).astype(jnp.bfloat16)
    return loss, grad_queries, grad_keys, grad_comp, grad_gain
```

```python
import functools

import jax
import jax.numpy as jnp
from jax import lax
from jax.experimental import pallas as pl
from jax.experimental.pallas import tpu as pltpu
from jax.sharding import PartitionSpec as P

DH = 128
HEADS = 8
KERNEL = 32
STRIDE = 16
LANES = 128
TILE = 64
TILE_UNROLL = 1
HEAD_UNROLL = 8

big_negative = -1e30
loss_scale = 256.0
f32 = jnp.float32
bf16 = jnp.bfloat16


def split3(x):
    first = x.astype(bf16)
    rest = x - first.astype(f32)
    second = rest.astype(bf16)
    third = (rest - second.astype(f32)).astype(bf16)
    return first, second, third


def remote(src, dst, send_sem, recv_sem, device):
    return pltpu.make_async_remote_copy(
        src_ref=src,
        dst_ref=dst,
        send_sem=send_sem,
        recv_sem=recv_sem,
        device_id={"ctx": device},
        device_id_type=pl.DeviceIdType.MESH,
    )


def loop(count, step, start):
    if count <= 4:
        for i in range(count):
            start = step(i, start)
        return start
    return lax.fori_loop(0, count, step, start)


def aligned(i, size):
    return pl.ds(pl.multiple_of(i * size, size), size)


def fold(x, op):
    rows, lanes = x.shape
    return op(x.reshape(rows // 8, 8, lanes), axis=0)


def kernel(
    n, gb, rc,
    slab_ref, keys_hbm, gain_hbm, w_hbm, q_hbm, t_hbm,
    loss_ref, gq_ref, gk_ref, gcomp_ref, ggain_ref,
    keys_ref, gain_ref, w_ref, q_v, t_v, pool_v, part_v, halo_v, pooled_v, comp_v, compt_v,
    bias_v, tp_v, s_v, g_v, pk_v, wt_v, lse_v, cv_v, p_v, pair_v, rs_v,
    co_v, ci_v, cs_v, cr_v, cg_v, gs_v, gf_v, gp_v, carry_v,
    local_sem, pool_s, pool_r, part_s, part_r, pair_s, pair_r, rs_s, rs_r, cr_s, cr_r, cg_s, cg_r, gs_s, gs_r, side_sem,
):
    me = lax.axis_index("ctx")
    rows, count = t_v.shape
    nb = count // n
    inv = DH ** (-0.5)
    core = lax.rem(me, 2)
    mine = lax.div(me, 2)
    half = n // 2
    twin = me + 1 - 2 * core
    upper = lax.div(mine, half // 2)
    far = (half - 1) * (1 - upper)
    toward = 2 * upper - 1

    def other_chips(act):
        def step(i, _):
            chip = far + toward * i

            @pl.when(chip != mine)
            def _():
                act(chip)

            return 0

        lax.fori_loop(0, half, step, 0)

    barrier = pltpu.get_barrier_semaphore()

    def signal(device):
        pl.semaphore_signal(
            barrier, inc=1, device_id={"ctx": device}, device_id_type=pl.DeviceIdType.MESH
        )

    def greet(chip):
        signal(2 * chip)
        signal(2 * chip + 1)

    other_chips(greet)
    signal(twin)

    q_copy = pltpu.make_async_copy(q_hbm, q_v, local_sem.at[0])
    t_copy = pltpu.make_async_copy(t_hbm, t_v, local_sem.at[1])
    keys_copy = pltpu.make_async_copy(keys_hbm, keys_ref, local_sem.at[3])
    gain_copy = pltpu.make_async_copy(gain_hbm, gain_ref, local_sem.at[4])
    w_copy = pltpu.make_async_copy(w_hbm, w_ref, local_sem.at[5])
    keys_copy.start()
    gain_copy.start()
    t_copy.start()
    w_copy.start()
    q_copy.start()

    keys_copy.wait()
    gain_copy.wait()
    keys3 = keys_ref[...].astype(f32).reshape(nb, STRIDE, DH)
    gain_lo = gain_ref[0:STRIDE, :]
    gain_hi = gain_ref[STRIDE:KERNEL, :]
    low = jnp.sum(keys3 * gain_lo[None], axis=1)
    high = jnp.sum(keys3 * gain_hi[None], axis=1)
    pool_v[me] = (low + jnp.concatenate([high[1:], high[:1]], axis=0)).astype(bf16)
    part_v[me, 0:1] = low[nb - 1 : nb]
    part_v[me, 1:2] = high[0:1]
    part_v[n] = jnp.zeros((8, DH), f32)

    @pl.when(me == n - 1)
    def _():
        halo_v[...] = jnp.zeros((STRIDE, DH), bf16)

    @pl.when(me == 0)
    def _():
        carry_v[...] = jnp.zeros((8, DH), f32)

    if rc < 8:
        cg_v[...] = jnp.zeros_like(cg_v)

    t_copy.wait()
    place0 = slab_ref[0] * rows

    def prepare(base):
        def first(c, total):
            for l0 in range(0, gb, LANES):
                teach = t_v[pl.ds(base + l0, LANES), aligned(c, LANES)].astype(f32).T
                end = STRIDE * (c * LANES + lax.broadcasted_iota(jnp.int32, (LANES, LANES), 0)) + (KERNEL - 1)
                place = place0 + base + l0 + lax.broadcasted_iota(jnp.int32, (LANES, LANES), 1)
                visible = end <= place
                seen = jnp.where(visible, teach, 0.0)
                bias_v[aligned(c, LANES), l0 : l0 + LANES] = jnp.where(visible, 0.0, big_negative)
                tp_v[aligned(c, LANES), l0 : l0 + LANES] = seen
                part = fold(seen, jnp.sum)
                total = total[:l0 // LANES] + (total[l0 // LANES] + part,) + total[l0 // LANES + 1 :]
            return total

        zero = jnp.zeros((8, LANES), f32)
        total8 = loop(count // LANES, first, (zero,) * (gb // LANES))
        kl8 = zero
        for l0 in range(0, gb, LANES):
            total = jnp.sum(total8[l0 // LANES], axis=0, keepdims=True)
            safe = jnp.where(total > 0, total, 1.0)
            shift = 3.0 - jnp.log2(safe)

            def second(c, acc):
                at = (aligned(c, LANES), slice(l0, l0 + LANES))
                seen = tp_v[at]
                tprob = seen / safe
                tp_v[at] = tprob
                return acc + fold(tprob * (jnp.log2(jnp.maximum(seen, 1e-30)) + shift), jnp.sum)

            kl8 = loop(count // LANES, second, kl8)
        return kl8

    whole = gb == rows
    kl_start = prepare(0) if whole else jnp.zeros((8, LANES), f32)

    pl.semaphore_wait(barrier, n - 1)

    def pool_copy(dst, slot):
        return remote(pool_v.at[slot], pool_v.at[slot], pool_s.at[dst], pool_r.at[slot], dst)

    def part_copy(dst, slot):
        pair = part_v.at[slot, pl.ds(0, 2)]
        return remote(pair, pair, part_s.at[dst], part_r.at[slot], dst)

    def send_pool(chip):
        for c in range(2):
            pool_copy(2 * chip + c, me).start()
            part_copy(2 * chip + c, me).start()

    other_chips(send_pool)
    pool_copy(twin, me).start()
    part_copy(twin, me).start()

    def halo_copy(dst):
        return remote(
            keys_ref.at[pl.ds(0, STRIDE)], halo_v, side_sem.at[0], side_sem.at[1], dst
        )

    @pl.when(me > 0)
    def _():
        halo_copy(me - 1).start()

    def take_pool(k, _):
        src = lax.rem(me + k, n)
        pool_copy(src, src).wait_recv()
        part_copy(src, src).wait_recv()
        return 0

    w_copy.wait()
    q_copy.wait()
    lax.fori_loop(1, n, take_pool, 0)
    last_row = lax.broadcasted_iota(jnp.int32, (n, nb, DH), 1) == nb - 1
    edges = part_v[0:n, 0:1, :] + part_v[1 : n + 1, 1:2, :]
    pooled = jnp.where(last_row, edges, pool_v[...].astype(f32)).astype(bf16)
    pooled_v[...] = pooled.reshape(half, 2, nb, DH)
    comp_v[...] = jnp.dot(
        pooled.reshape(count, DH), w_ref[...], preferred_element_type=f32
    ).astype(bf16)

    nt = (((1,), (1,)), ((), ()))
    tn = (((0,), (0,)), ((), ()))
    to_log2 = inv * 1.4426950408889634

    def probabilities(base, kl8):
        queries_at = pl.ds(base, gb)

        def head(h, _):
            qh = q_v[queries_at, aligned(h, DH)]

            def scores(c, top):
                s = lax.dot_general(
                    comp_v[aligned(c, LANES), :], qh, nt, preferred_element_type=f32
                )
                s = s * to_log2 + bias_v[aligned(c, LANES), :]
                s_v[h, aligned(c, LANES), :] = s
                return jnp.maximum(top, fold(s, jnp.max))

            top8 = loop(count // LANES, scores, jnp.full((8, gb), 2 * big_negative, f32))
            top = jnp.max(top8, axis=0, keepdims=True)

            def sums(c, total):
                return total + fold(jnp.exp2(s_v[h, aligned(c, LANES), :] - top), jnp.sum)

            total8 = loop(count // LANES, sums, jnp.zeros((8, gb), f32))
            total = jnp.sum(total8, axis=0, keepdims=True)
            lse = jnp.where(top > 0.5 * big_negative, top + jnp.log2(total), 0.0)
            lse_v[h] = jnp.broadcast_to(lse, (8, gb))
            return 0

        lax.fori_loop(0, HEADS, head, 0, unroll=HEAD_UNROLL)

        for l0 in range(0, gb, LANES):
            lanes = slice(l0, l0 + LANES)

            def ratios(c, carry):
                kl8, cv = carry
                at = aligned(c, TILE)
                x = []
                for h in range(HEADS):
                    x.append((s_v[h, at, lanes].reshape(TILE // 8, 8, LANES) - lse_v[h, :, lanes][None]))
                tops = x
                while len(tops) > 1:
                    tops = [jnp.maximum(a, b) for a, b in zip(tops[::2], tops[1::2])]
                peak = tops[0]
                u = [jnp.exp2(a - peak) for a in x]
                mass = u
                while len(mass) > 1:
                    mass = [a + b for a, b in zip(mass[::2], mass[1::2])]
                mass = mass[0]
                tprob = tp_v[at, lanes].reshape(TILE // 8, 8, LANES)
                weight = tprob / mass
                kl8 = kl8 - jnp.sum(tprob * (peak + jnp.log2(mass)), axis=0)
                pk_v[at, lanes] = jnp.exp2(peak).reshape(TILE, LANES)
                wt_v[at, lanes] = (loss_scale * weight).reshape(TILE, LANES)
                for h in range(HEADS):
                    s_v[h, at, lanes] = u[h].reshape(TILE, LANES)
                cv = tuple(a + jnp.sum(b * weight, axis=0) for a, b in zip(cv, u))
                return kl8, cv

            zero = jnp.zeros((8, LANES), f32)
            kl8, cv = lax.fori_loop(
                0, count // TILE, ratios, (kl8, (zero,) * HEADS), unroll=TILE_UNROLL
            )
            for h in range(HEADS):
                total = loss_scale * jnp.sum(cv[h], axis=0, keepdims=True)
                cv_v[h, :, lanes] = jnp.broadcast_to(total, (8, LANES))
        return kl8

    def block_grads(base, i, first):
        c = first_chunk + chunk_step * i
        at = aligned(c, LANES)
        acc = jnp.zeros((LANES, DH), f32)
        peak = pk_v[at, :].reshape(LANES // 8, 8, gb)
        weight = wt_v[at, :].reshape(LANES // 8, 8, gb)
        for h in range(HEADS):
            u = s_v[h, at, :].reshape(LANES // 8, 8, gb)
            g = (u * (peak * cv_v[h][None] - weight)).reshape(LANES, gb).astype(bf16)
            g_v[h, at, :] = g
            acc = acc + jnp.dot(
                g, q_v[pl.ds(base, gb), h * DH : (h + 1) * DH], preferred_element_type=f32
            )
        acc = acc * inv
        for k in range(LANES // nb):
            where = (k % 2, c * (LANES // nb // 2) + k // 2)
            if first:
                p_v[where] = acc[k * nb : (k + 1) * nb]
            else:
                p_v[where] = p_v[where] + acc[k * nb : (k + 1) * nb]
        return c

    def query_grads(base, h0, h1):
        def head(h, _):
            gq = jnp.dot(compt_v[...], g_v[h], preferred_element_type=f32) * inv
            gq_ref[pl.ds(base, gb), aligned(h, DH)] = gq.T.astype(bf16)
            return 0

        lax.fori_loop(h0, h1, head, 0)

    def pair_copy(slot):
        return remote(
            p_v.at[1 - core, slot], pair_v.at[slot], pair_s.at[slot], pair_r.at[slot], twin
        )

    def rs_copy(dst, slot):
        return remote(
            p_v.at[core, dst], rs_v.at[slot], rs_s.at[dst], rs_r.at[slot], 2 * dst + core
        )

    chunks = count // LANES
    per_chunk = LANES // nb // 2
    first_chunk = (chunks - 1) * (1 - upper)
    chunk_step = toward

    if whole:
        kl8 = probabilities(0, kl_start)

        def chunk(i, _):
            c = block_grads(0, i, True)
            for k in range(per_chunk):
                pair_copy(c * per_chunk + k).start()
            return 0

        lax.fori_loop(0, chunks, chunk, 0)
        compt_v[...] = comp_v[...].astype(f32).T.astype(bf16)
    else:
        compt_v[...] = comp_v[...].astype(f32).T.astype(bf16)
        p_v[...] = jnp.zeros_like(p_v)

        def block_step(base):
            def chunk(i, _):
                block_grads(base, i, False)
                return 0

            lax.fori_loop(0, chunks, chunk, 0)

        def group(i, kl8):
            base = pl.multiple_of(i * gb, gb)
            kl8 = probabilities(base, kl8 + prepare(base))
            block_step(base)
            query_grads(base, 0, HEADS)
            return kl8

        kl8 = lax.fori_loop(0, rows // gb, group, kl_start)

        def send_pair(slot, _):
            pair_copy(slot).start()
            return 0

        lax.fori_loop(0, half, send_pair, 0)

    def forward(chip):
        pair_copy(chip).wait_recv()
        p_v[core, chip] = p_v[core, chip] + pair_v[chip]
        rs_copy(chip, mine).start()

    other_chips(forward)
    pair_copy(mine).wait_recv()
    own_sum = p_v[core, mine] + pair_v[mine]
    p_v[core, mine] = own_sum
    rs_v[mine] = own_sum

    sums3 = split3(p_v[core].reshape(half * nb, DH))
    pooled_half = pooled_v[:, pl.ds(core, 1)].reshape(half * nb, DH)
    comp_part = lax.dot_general(
        jnp.concatenate([pooled_half] * 3, axis=0),
        jnp.concatenate(sums3[::-1], axis=0),
        tn,
        preferred_element_type=f32,
    )
    kl_total = jnp.sum(jnp.sum(kl8, axis=0, keepdims=True), axis=1, keepdims=True)
    kl_rows = jnp.broadcast_to(kl_total * 0.6931471805599453, (8, DH))
    hr = DH // 2
    for c in range(2):
        co_v[c, 0:hr] = comp_part[c * hr : (c + 1) * hr]
        co_v[c, hr : hr + 8] = kl_rows

    def cx_copy():
        return remote(co_v.at[1 - core], ci_v, side_sem.at[4], side_sem.at[5], twin)

    cx_copy().start()
    if whole:
        query_grads(0, 0, HEADS // 2)
    cx_copy().wait_recv()
    comp_sum = co_v[core] + ci_v[...]
    slot_rows = cs_v.shape[1]
    for d in range(half):
        if (d + 1) * rc <= hr:
            cs_v[d] = jnp.concatenate(
                [comp_sum[d * rc : (d + 1) * rc], comp_sum[hr : hr + slot_rows - rc]], axis=0
            )
        else:
            cs_v[d] = jnp.broadcast_to(comp_sum[hr : hr + 1], (slot_rows, DH))

    def cr_copy(dst, slot):
        used = pl.ds(0, rc + 1)
        return remote(
            cs_v.at[dst, used], cr_v.at[slot, used], cr_s.at[dst], cr_r.at[slot], 2 * dst + core
        )

    other_chips(lambda chip: cr_copy(chip, mine).start())
    cr_v[mine] = cs_v[mine]
    if whole:
        query_grads(0, HEADS // 2, HEADS)

    @pl.when(me < n - 1)
    def _():
        halo_copy(me).wait_recv()

    upper3 = jnp.concatenate(
        [keys3[1:], halo_v[...].astype(f32).reshape(1, STRIDE, DH)], axis=0
    )

    other_chips(lambda chip: rs_copy(chip, chip).wait_recv())
    own = lax.fori_loop(1, half, lambda d, total: total + rs_v[d], rs_v[0])
    own3 = split3(own)
    gp3 = lax.dot_general(
        jnp.concatenate(own3, axis=0), w_ref[...], nt, preferred_element_type=f32
    )
    grad_pooled = (gp3[2 * nb :] + gp3[nb : 2 * nb]) + gp3[:nb]
    gp_v[...] = grad_pooled

    def carry_copy(dst):
        return remote(
            gp_v.at[pl.ds(nb - 8, 8)], carry_v, side_sem.at[2], side_sem.at[3], dst
        )

    gs_v[mine] = jnp.concatenate(
        [
            jnp.sum(grad_pooled[:, None, :] * keys3, axis=0),
            jnp.sum(grad_pooled[:, None, :] * upper3, axis=0),
        ],
        axis=0,
    )

    def gs_copy(dst, slot):
        return remote(
            gs_v.at[slot], gs_v.at[slot], gs_s.at[dst], gs_r.at[slot], 2 * dst + core
        )

    other_chips(lambda chip: gs_copy(chip, mine).start())

    @pl.when(me < n - 1)
    def _():
        carry_copy(me + 1).start()

    other_chips(lambda chip: cr_copy(chip, chip).wait_recv())
    comp_out = lax.fori_loop(1, half, lambda d, total: total + cr_v[d], cr_v[0])
    cg_v[core, mine, 0:rc] = comp_out[0:rc]
    loss_ref[...] = comp_out[rc : rc + 1] * (1.0 / (rows * n))

    def cg_copy(dst, slot):
        piece = cg_v.at[core, slot, pl.ds(0, rc)]
        return remote(piece, piece, cg_s.at[dst], cg_r.at[slot], 2 * dst + core)

    other_chips(lambda chip: cg_copy(chip, mine).start())

    @pl.when(me > 0)
    def _():
        carry_copy(me).wait_recv()

    before = jnp.concatenate([carry_v[7:8, :], grad_pooled[: nb - 1]], axis=0)
    grad_keys = grad_pooled[:, None, :] * gain_lo[None] + before[:, None, :] * gain_hi[None]
    gk_ref[...] = grad_keys.reshape(nb * STRIDE, DH).astype(bf16)

    def drop_pool(k, _):
        dst = lax.rem(me + k, n)
        pool_copy(dst, me).wait_send()
        part_copy(dst, me).wait_send()
        return 0

    lax.fori_loop(1, n, drop_pool, 0)

    def drop_chip(chip):
        pair_copy(chip).wait_send()
        rs_copy(chip, mine).wait_send()
        cr_copy(chip, mine).wait_send()

    other_chips(drop_chip)
    pair_copy(mine).wait_send()
    cx_copy().wait_send()

    @pl.when(me > 0)
    def _():
        halo_copy(me - 1).wait_send()

    @pl.when(me < n - 1)
    def _():
        carry_copy(me + 1).wait_send()

    other_chips(lambda chip: cg_copy(chip, chip).wait_recv())

    def cf_copy(slot):
        return remote(cg_v.at[slot], cg_v.at[slot], side_sem.at[6], side_sem.at[7], twin)

    cf_copy(core).start()
    other_chips(lambda chip: gs_copy(chip, chip).wait_recv())
    gain_sum = lax.fori_loop(1, half, lambda d, total: total + gs_v[d], gs_v[0])
    gf_v[0] = gain_sum

    def gf_copy():
        return remote(gf_v.at[0], gf_v.at[1], side_sem.at[8], side_sem.at[9], twin)

    gf_copy().start()

    def drop_last(chip):
        cg_copy(chip, mine).wait_send()
        gs_copy(chip, mine).wait_send()

    other_chips(drop_last)
    cf_copy(1 - core).wait_recv()
    cf_copy(core).wait_send()
    for c in range(2):
        for d in range(half):
            if (d + 1) * rc <= hr:
                gcomp_ref[c * hr + d * rc : c * hr + (d + 1) * rc, :] = cg_v[c, d, 0:rc]
    gf_copy().wait_recv()
    ggain_ref[...] = gain_sum + gf_v[1]
    gf_copy().wait_send()


def finish(*refs):
    sources, targets, sem = refs[:5], refs[5:10], refs[10]
    copies = [
        pltpu.make_async_copy(source, target, sem.at[i])
        for i, (source, target) in enumerate(zip(sources, targets))
    ]
    for copy in copies:
        copy.start()
    for copy in copies:
        copy.wait()


def body(n, keys, queries, teacher_map, slab_index, pos_gain, w_comp):
    rows, count = teacher_map.shape
    nb = count // n
    half = n // 2
    gb = rows if count <= 1024 else min(rows, LANES)
    rc = -(-(DH // 2) // half)
    slot_rows = -(-(rc + 1) // 8) * 8
    dma = pltpu.SemaphoreType.DMA
    vmem = pl.BlockSpec(memory_space=pltpu.VMEM)
    hbm = pl.BlockSpec(memory_space=pltpu.HBM)
    shapes = (
            jax.ShapeDtypeStruct((1, DH), f32),
            jax.ShapeDtypeStruct((rows, HEADS * DH), bf16),
            jax.ShapeDtypeStruct(keys.shape, bf16),
            jax.ShapeDtypeStruct((DH, DH), f32),
            jax.ShapeDtypeStruct((KERNEL, DH), f32),
        )
    results = pl.pallas_call(
        functools.partial(kernel, n, gb, rc),
        out_shape=shapes,
        in_specs=[pl.BlockSpec(memory_space=pltpu.SMEM)] + [hbm] * 5,
        out_specs=(vmem,) * 5,
        scratch_shapes=[
            pltpu.VMEM(keys.shape, bf16),
            pltpu.VMEM(pos_gain.shape, f32),
            pltpu.VMEM(w_comp.shape, bf16),
            pltpu.VMEM((rows, HEADS * DH), bf16),
            pltpu.VMEM((rows, count), bf16),
            pltpu.VMEM((n, nb, DH), bf16),
            pltpu.VMEM((n + 1, 8, DH), f32),
            pltpu.VMEM((STRIDE, DH), bf16),
            pltpu.VMEM((half, 2, nb, DH), bf16),
            pltpu.VMEM((count, DH), bf16),
            pltpu.VMEM((DH, count), bf16),
            pltpu.VMEM((count, gb), f32),
            pltpu.VMEM((count, gb), f32),
            pltpu.VMEM((HEADS, count, gb), f32),
            pltpu.VMEM((HEADS, count, gb), bf16),
            pltpu.VMEM((count, gb), f32),
            pltpu.VMEM((count, gb), f32),
            pltpu.VMEM((HEADS, 8, gb), f32),
            pltpu.VMEM((HEADS, 8, gb), f32),
            pltpu.VMEM((2, half, nb, DH), f32),
            pltpu.VMEM((half, nb, DH), f32),
            pltpu.VMEM((half, nb, DH), f32),
            pltpu.VMEM((2, DH // 2 + 8, DH), f32),
            pltpu.VMEM((DH // 2 + 8, DH), f32),
            pltpu.VMEM((half, slot_rows, DH), f32),
            pltpu.VMEM((half, slot_rows, DH), f32),
            pltpu.VMEM((2, half, max(rc, 8), DH), f32),
            pltpu.VMEM((half, KERNEL, DH), f32),
            pltpu.VMEM((2, KERNEL, DH), f32),
            pltpu.VMEM((nb, DH), f32),
            pltpu.VMEM((8, DH), f32),
            dma((6,)),
        ]
        + [dma((n,))] * 4
        + [dma((half,))] * 10
        + [dma((10,))],
        compiler_params=pltpu.CompilerParams(
            collective_id=0, has_side_effects=True, vmem_limit_bytes=(24 if gb == rows else 56) * 1024 * 1024
        ),
    )(slab_index, *[pltpu.with_memory_space_constraint(x, pltpu.HBM) for x in (keys, pos_gain, w_comp, queries, teacher_map)])
    any_space = pl.BlockSpec(memory_space=pl.ANY)
    loss, gq, gk, gcomp, ggain = pl.pallas_call(
        finish,
        out_shape=shapes,
        in_specs=[any_space] * 5,
        out_specs=[any_space] * 5,
        scratch_shapes=[dma((5,))],
        compiler_params=pltpu.CompilerParams(vmem_limit_bytes=4 * 1024 * 1024),
    )(*results)
    return (loss[0, 0:1], gq, gk, gcomp, ggain)


def solution(mesh):
    in_specs = (
        P(("groups", "ctx"), None),
        P(("groups", "ctx"), None),
        P(("groups", "ctx"), None),
        P(("groups", "ctx")),
        P(),
        P(),
    )
    out_specs = (
        P("groups"),
        P(("groups", "ctx"), None),
        P(("groups", "ctx"), None),
        P("groups", None),
        P("groups", None),
    )
    return jax.shard_map(
        functools.partial(body, mesh.shape["ctx"]),
        mesh=mesh, in_specs=in_specs, out_specs=out_specs, check_vma=False,
    )
```

```python
import functools

import jax
import jax.numpy as jnp
from jax import lax
from jax.experimental import pallas as pl
from jax.experimental.pallas import tpu as pltpu
from jax.sharding import PartitionSpec as P

DH = 128
HEADS = 8
KERNEL = 32
STRIDE = 16
LANES = 128
TILE = 16
TILE_UNROLL = 8
HEAD_UNROLL = 8
GQ_UNROLL = 4
CHUNK_UNROLL = 4

big_negative = -1e30
loss_scale = 256.0
f32 = jnp.float32
bf16 = jnp.bfloat16


def split3(x):
    first = x.astype(bf16)
    rest = x - first.astype(f32)
    second = rest.astype(bf16)
    third = (rest - second.astype(f32)).astype(bf16)
    return first, second, third


def remote(src, dst, send_sem, recv_sem, device):
    return pltpu.make_async_remote_copy(
        src_ref=src,
        dst_ref=dst,
        send_sem=send_sem,
        recv_sem=recv_sem,
        device_id={"ctx": device},
        device_id_type=pl.DeviceIdType.MESH,
    )


def loop(count, step, start):
    if count <= 4:
        for i in range(count):
            start = step(i, start)
        return start
    return lax.fori_loop(0, count, step, start)


def aligned(i, size):
    return pl.ds(pl.multiple_of(i * size, size), size)


def fold(x, op):
    rows, lanes = x.shape
    return op(x.reshape(rows // 8, 8, lanes), axis=0)


def kernel(
    n, gb, rc,
    slab_ref, keys_hbm, gain_hbm, w_hbm, q_hbm, t_hbm,
    loss_ref, gq_ref, gk_ref, gcomp_ref, ggain_ref,
    keys_ref, gain_ref, w_ref, q_v, t_v, pool_v, halo_v, pooled_v, comp_v, compt_v,
    bias_v, tp_v, s_v, u_v, g_v, qs_v, pk_v, wt_v, lse_v, cv_v, p_v, pair_v, rs_v,
    gs_v, gf_v, gp_v, carry_v,
    local_sem, pair_s, pair_r, all_sem, side_sem,
):
    me = lax.axis_index("ctx")
    rows, count = t_v.shape
    nb = count // n
    inv = DH ** (-0.5)
    core = lax.rem(me, 2)
    mine = lax.div(me, 2)
    half = n // 2
    twin = me + 1 - 2 * core
    upper = lax.div(mine, half // 2)
    far = (half - 1) * (1 - upper)
    toward = 2 * upper - 1

    def other_chips(act):
        def step(i, _):
            chip = far + toward * i

            @pl.when(chip != mine)
            def _():
                act(chip)

            return 0

        lax.fori_loop(0, half, step, 0)

    barrier = pltpu.get_barrier_semaphore()

    def signal(device):
        pl.semaphore_signal(
            barrier, inc=1, device_id={"ctx": device}, device_id_type=pl.DeviceIdType.MESH
        )

    def greet(chip):
        signal(2 * chip)
        signal(2 * chip + 1)

    other_chips(greet)
    signal(twin)

    q_copy = pltpu.make_async_copy(q_hbm, q_v, local_sem.at[0])
    t_copy = pltpu.make_async_copy(t_hbm, t_v, local_sem.at[1])
    keys_copy = pltpu.make_async_copy(keys_hbm, keys_ref, local_sem.at[3])
    gain_copy = pltpu.make_async_copy(gain_hbm, gain_ref, local_sem.at[4])
    w_copy = pltpu.make_async_copy(w_hbm, w_ref, local_sem.at[5])
    keys_copy.start()
    gain_copy.start()
    t_copy.start()
    w_copy.start()
    q_copy.start()

    keys_copy.wait()
    gain_copy.wait()
    keys3 = keys_ref[...].astype(f32).reshape(nb, STRIDE, DH)
    gain_lo = gain_ref[0:STRIDE, :]
    gain_hi = gain_ref[STRIDE:KERNEL, :]
    low = jnp.sum(keys3 * gain_lo[None], axis=1)
    high = jnp.sum(keys3 * gain_hi[None], axis=1)
    pool_v[mine, core, 0:nb] = (low + jnp.concatenate([high[1:], high[:1]], axis=0)).astype(bf16)
    pool_v[mine, core, nb : nb + 16] = jnp.concatenate(
        [*split3(low[nb - 1 : nb]), *split3(high[0:1]), jnp.zeros((10, DH), bf16)], axis=0
    )
    @pl.when(me == n - 1)
    def _():
        halo_v[...] = jnp.zeros((STRIDE, DH), bf16)

    @pl.when(me == 0)
    def _():
        carry_v[...] = jnp.zeros((8, DH), f32)

    t_copy.wait()
    place0 = slab_ref[0] * rows

    def prepare(base):
        def first(c, total):
            for l0 in range(0, gb, LANES):
                teach = t_v[pl.ds(base + l0, LANES), aligned(c, LANES)].astype(f32).T
                end = STRIDE * (c * LANES + lax.broadcasted_iota(jnp.int32, (LANES, LANES), 0)) + (KERNEL - 1)
                place = place0 + base + l0 + lax.broadcasted_iota(jnp.int32, (LANES, LANES), 1)
                visible = end <= place
                seen = jnp.where(visible, teach, 0.0)
                bias_v[aligned(c, LANES), l0 : l0 + LANES] = jnp.where(visible, 0.0, big_negative)
                tp_v[aligned(c, LANES), l0 : l0 + LANES] = seen
                part = fold(seen, jnp.sum)
                total = total[:l0 // LANES] + (total[l0 // LANES] + part,) + total[l0 // LANES + 1 :]
            return total

        zero = jnp.zeros((8, LANES), f32)
        total8 = loop(count // LANES, first, (zero,) * (gb // LANES))
        kl8 = zero
        for l0 in range(0, gb, LANES):
            total = jnp.sum(total8[l0 // LANES], axis=0, keepdims=True)
            safe = jnp.where(total > 0, total, 1.0)
            shift = 3.0 - jnp.log2(safe)

            def second(c, acc):
                at = (aligned(c, LANES), slice(l0, l0 + LANES))
                seen = tp_v[at]
                tprob = seen / safe
                tp_v[at] = tprob
                return acc + fold(tprob * (jnp.log2(jnp.maximum(seen, 1e-30)) + shift), jnp.sum)

            kl8 = loop(count // LANES, second, kl8)
        return kl8

    def stack(base):
        for h in range(HEADS):
            qs_v[h * gb : (h + 1) * gb, :] = q_v[pl.ds(base, gb), h * DH : (h + 1) * DH]

    whole = gb == rows
    e_v = u_v if whole else s_v
    kl_start = prepare(0) if whole else jnp.zeros((8, LANES), f32)

    pl.semaphore_wait(barrier, n - 1)

    def pool_copy(chip):
        block = pool_v.at[mine, core]
        return remote(block, block, all_sem.at[0], all_sem.at[1], 2 * chip + core)

    def relay_copy(c):
        blocks = pool_v.at[:, c]
        return remote(blocks, blocks, side_sem.at[8], side_sem.at[9], twin)

    def wait_bytes(ref, sem):
        pltpu.make_async_copy(ref, ref, sem).wait()

    other_chips(lambda chip: pool_copy(chip).start())

    def halo_copy(dst):
        return remote(
            keys_ref.at[pl.ds(0, STRIDE)], halo_v, side_sem.at[0], side_sem.at[1], dst
        )

    @pl.when(me > 0)
    def _():
        halo_copy(me - 1).start()

    w_copy.wait()
    q_copy.wait()
    if whole:
        stack(0)
    wait_bytes(pool_v.at[pl.ds(0, half - 1), 0], all_sem.at[1])
    relay_copy(core).start()
    relay_copy(1 - core).wait_recv()
    blocks = pool_v[...].reshape(n, nb + 16, DH)
    last_row = lax.broadcasted_iota(jnp.int32, (n, nb, DH), 1) == nb - 1
    ends = blocks[:, nb : nb + 16, :].astype(f32)
    low_end = (ends[:, 2:3] + ends[:, 1:2]) + ends[:, 0:1]
    high_end = (ends[:, 5:6] + ends[:, 4:5]) + ends[:, 3:4]
    edges = low_end + jnp.concatenate(
        [high_end[1:], jnp.zeros((1, 1, DH), f32)], axis=0
    )
    pooled = jnp.where(last_row, edges, blocks[:, 0:nb, :].astype(f32)).astype(bf16)
    pooled_v[...] = pooled.reshape(count, DH)
    comp_v[...] = jnp.dot(
        pooled_v[...], w_ref[...], preferred_element_type=f32
    ).astype(bf16)

    nt = (((1,), (1,)), ((), ()))
    tn = (((0,), (0,)), ((), ()))
    to_log2 = inv * 1.4426950408889634

    def probabilities(base, kl8):
        queries_at = pl.ds(base, gb)

        def head(h, _):
            qh = q_v[queries_at, aligned(h, DH)]

            def scores(c, top):
                s = lax.dot_general(
                    comp_v[aligned(c, LANES), :], qh, nt, preferred_element_type=f32
                )
                s = s * to_log2 + bias_v[aligned(c, LANES), :]
                s_v[h, aligned(c, LANES), :] = s
                return jnp.maximum(top, fold(s, jnp.max))

            top8 = loop(count // LANES, scores, jnp.full((8, gb), 2 * big_negative, f32))
            top = jnp.max(top8, axis=0, keepdims=True)

            def sums(c, total):
                return total + fold(jnp.exp2(s_v[h, aligned(c, LANES), :] - top), jnp.sum)

            total8 = loop(count // LANES, sums, jnp.zeros((8, gb), f32))
            total = jnp.sum(total8, axis=0, keepdims=True)
            lse = jnp.where(top > 0.5 * big_negative, top + jnp.log2(total), 0.0)
            lse_v[h] = jnp.broadcast_to(lse, (8, gb))
            return 0

        lax.fori_loop(0, HEADS, head, 0, unroll=HEAD_UNROLL)

        for l0 in range(0, gb, LANES):
            lanes = slice(l0, l0 + LANES)
            lse = [lse_v[h, :, lanes][None] for h in range(HEADS)]

            def ratios(c, carry):
                kl8, cv = carry
                at = aligned(c, TILE)
                x = []
                for h in range(HEADS):
                    x.append((s_v[h, at, lanes].reshape(TILE // 8, 8, LANES) - lse[h]))
                tops = x
                while len(tops) > 1:
                    tops = [jnp.maximum(a, b) for a, b in zip(tops[::2], tops[1::2])]
                peak = tops[0]
                u = [jnp.exp2(a - peak) for a in x]
                mass = u
                while len(mass) > 1:
                    mass = [a + b for a, b in zip(mass[::2], mass[1::2])]
                mass = mass[0]
                tprob = tp_v[at, lanes].reshape(TILE // 8, 8, LANES)
                weight = tprob / mass
                kl8 = kl8 - jnp.sum(tprob * (peak + jnp.log2(mass)), axis=0)
                pk_v[at, lanes] = jnp.exp2(peak).reshape(TILE, LANES)
                wt_v[at, lanes] = (loss_scale * weight).reshape(TILE, LANES)
                for h in range(HEADS):
                    e_v[h, at, lanes] = u[h].reshape(TILE, LANES)
                cv = tuple(a + jnp.sum(b * weight, axis=0) for a, b in zip(cv, u))
                return kl8, cv

            zero = jnp.zeros((8, LANES), f32)
            kl8, cv = lax.fori_loop(
                0, count // TILE, ratios, (kl8, (zero,) * HEADS), unroll=TILE_UNROLL
            )
            for h in range(HEADS):
                total = loss_scale * jnp.sum(cv[h], axis=0, keepdims=True)
                cv_v[h, :, lanes] = jnp.broadcast_to(total, (8, LANES))
        return kl8

    def block_grads(base, i, first, comp_part):
        c = first_chunk + chunk_step * i
        at = aligned(c, LANES)
        peak = pk_v[at, :].reshape(LANES // 8, 8, gb)
        weight = wt_v[at, :].reshape(LANES // 8, 8, gb)
        for h in range(HEADS):
            u = e_v[h, at, :].reshape(LANES // 8, 8, gb)
            g = u * (peak * cv_v[h][None] - weight)
            g_v[at, h * gb : (h + 1) * gb] = g.reshape(LANES, gb).astype(bf16)
        acc = jnp.dot(g_v[at, :], qs_v[...], preferred_element_type=f32)
        acc = acc * inv
        for k in range(LANES // nb):
            where = (k % 2, c * (LANES // nb // 2) + k // 2)
            if first:
                p_v[where + (slice(0, nb),)] = acc[k * nb : (k + 1) * nb]
            else:
                p_v[where + (slice(0, nb),)] += acc[k * nb : (k + 1) * nb]
        pieces = split3(acc)
        block = pooled_v[aligned(c, LANES), :]
        add = lax.dot_general(
            jnp.concatenate([block] * 3, axis=0),
            jnp.concatenate(pieces[::-1], axis=0),
            tn,
            preferred_element_type=f32,
        )
        return c, comp_part + add

    def query_grads(base, h0, h1):
        def head(h, _):
            gq = jnp.dot(compt_v[...], g_v[:, aligned(h, gb)], preferred_element_type=f32) * inv
            gq_ref[pl.ds(base, gb), aligned(h, DH)] = gq.T.astype(bf16)
            return 0

        lax.fori_loop(h0, h1, head, 0, unroll=GQ_UNROLL)

    used = nb + rc + 1

    def pair_copy(c):
        at = (pl.ds(c * per_chunk, per_chunk), pl.ds(0, nb))
        return remote(
            p_v.at[(1 - core,) + at], pair_v.at[at], pair_s.at[c], pair_r.at[c], twin
        )

    def side_copy():
        at = (slice(None), pl.ds(nb, rc + 1))
        return remote(
            p_v.at[(1 - core,) + at], pair_v.at[at], side_sem.at[4], side_sem.at[5], twin
        )

    def rs_copy(dst):
        at = pl.ds(0, used)
        return remote(
            p_v.at[core, dst, at], rs_v.at[mine, at], all_sem.at[2], all_sem.at[3], 2 * dst + core
        )

    chunks = count // LANES
    per_chunk = LANES // nb // 2
    first_chunk = (chunks - 1) * (1 - upper)
    chunk_step = toward

    no_part = jnp.zeros((DH, DH), f32)
    if whole:
        kl8 = probabilities(0, kl_start)

        def chunk(i, part):
            c, part = block_grads(0, i, True, part)
            pair_copy(c).start()
            return part

        comp_part = lax.fori_loop(0, chunks, chunk, no_part, unroll=CHUNK_UNROLL)
    else:
        compt_v[...] = comp_v[...].astype(f32).T.astype(bf16)
        p_v[...] = jnp.zeros_like(p_v)

        def group(i, carry):
            kl8, part = carry
            base = pl.multiple_of(i * gb, gb)
            stack(base)
            kl8 = probabilities(base, kl8 + prepare(base))
            part = lax.fori_loop(0, chunks, lambda k, a: block_grads(base, k, False, a)[1], part)
            query_grads(base, 0, HEADS)
            return kl8, part

        kl8, comp_part = lax.fori_loop(0, rows // gb, group, (kl_start, no_part))

        def send_pair(c, _):
            pair_copy(c).start()
            return 0

        lax.fori_loop(0, chunks, send_pair, 0)

    kl_total = jnp.sum(jnp.sum(kl8, axis=0, keepdims=True), axis=1, keepdims=True)
    kl_row = jnp.broadcast_to(kl_total * 0.6931471805599453, (1, DH))
    hr = DH // 2
    for c in range(2):
        for d in range(half):
            if (d + 1) * rc <= hr:
                p_v[c, d, nb : nb + rc] = comp_part[c * hr + d * rc : c * hr + (d + 1) * rc]
            else:
                p_v[c, d, nb : nb + rc] = jnp.zeros((rc, DH), f32)
            p_v[c, d, nb + rc : used] = kl_row

    side_copy().start()
    if whole:
        compt_v[...] = comp_v[...].astype(f32).T.astype(bf16)

    def forward(i, _):
        c = first_chunk + chunk_step * i
        pair_copy(c).wait_recv()

        @pl.when(i == 0)
        def _():
            side_copy().wait_recv()

        for k in range(per_chunk):
            chip = c * per_chunk + k
            total = p_v[core, chip, 0:used] + pair_v[chip, 0:used]

            @pl.when(chip != mine)
            def _():
                p_v[core, chip, 0:used] = total
                rs_copy(chip).start()

            @pl.when(chip == mine)
            def _():
                rs_v[mine, 0:used] = total

        return 0

    lax.fori_loop(0, chunks, forward, 0)
    if whole:
        query_grads(0, 0, HEADS)

    @pl.when(me < n - 1)
    def _():
        halo_copy(me).wait_recv()

    upper3 = jnp.concatenate(
        [keys3[1:], halo_v[...].astype(f32).reshape(1, STRIDE, DH)], axis=0
    )

    wait_bytes(rs_v.at[pl.ds(0, half - 1), pl.ds(0, used)], all_sem.at[3])
    sums = lax.fori_loop(
        1, half, lambda d, total: total + rs_v[d, 0:used], rs_v[0, 0:used]
    )
    own = sums[0:nb]
    own3 = split3(own)
    gp3 = lax.dot_general(
        jnp.concatenate(own3, axis=0), w_ref[...], nt, preferred_element_type=f32
    )
    grad_pooled = (gp3[2 * nb :] + gp3[nb : 2 * nb]) + gp3[:nb]
    gp_v[...] = grad_pooled

    def carry_copy(dst):
        return remote(
            gp_v.at[pl.ds(nb - 8, 8)], carry_v, side_sem.at[2], side_sem.at[3], dst
        )

    gs_v[mine, 0:KERNEL] = jnp.concatenate(
        [
            jnp.sum(grad_pooled[:, None, :] * keys3, axis=0),
            jnp.sum(grad_pooled[:, None, :] * upper3, axis=0),
        ],
        axis=0,
    )
    gs_v[mine, KERNEL : KERNEL + rc] = sums[nb : nb + rc]
    loss_ref[...] = sums[nb + rc : used] * (1.0 / (rows * n))

    def gs_copy(dst):
        piece = gs_v.at[mine, pl.ds(0, KERNEL + rc)]
        return remote(piece, piece, all_sem.at[4], all_sem.at[5], 2 * dst + core)

    other_chips(lambda chip: gs_copy(chip).start())

    @pl.when(me < n - 1)
    def _():
        carry_copy(me + 1).start()

    @pl.when(me > 0)
    def _():
        carry_copy(me).wait_recv()

    before = jnp.concatenate([carry_v[7:8, :], grad_pooled[: nb - 1]], axis=0)
    grad_keys = grad_pooled[:, None, :] * gain_lo[None] + before[:, None, :] * gain_hi[None]
    gk_ref[...] = grad_keys.reshape(nb * STRIDE, DH).astype(bf16)

    wait_bytes(pool_v.at[pl.ds(0, half - 1), 0], all_sem.at[0])
    relay_copy(core).wait_send()
    wait_bytes(rs_v.at[pl.ds(0, half - 1), pl.ds(0, used)], all_sem.at[2])

    def drop_pair(c, _):
        pair_copy(c).wait_send()
        return 0

    lax.fori_loop(0, chunks, drop_pair, 0)
    side_copy().wait_send()

    @pl.when(me > 0)
    def _():
        halo_copy(me - 1).wait_send()

    @pl.when(me < n - 1)
    def _():
        carry_copy(me + 1).wait_send()

    wait_bytes(gs_v.at[pl.ds(0, half - 1), pl.ds(0, KERNEL + rc)], all_sem.at[5])
    gf_v[core, 0:KERNEL] = lax.fori_loop(
        1, half, lambda d, total: total + gs_v[d, 0:KERNEL], gs_v[0, 0:KERNEL]
    )
    for d in range(half):
        if (d + 1) * rc <= hr:
            gf_v[core, KERNEL + d * rc : KERNEL + (d + 1) * rc] = gs_v[d, KERNEL : KERNEL + rc]

    def gf_copy(slot):
        return remote(gf_v.at[slot], gf_v.at[slot], side_sem.at[6], side_sem.at[7], twin)

    gf_copy(core).start()
    wait_bytes(gs_v.at[pl.ds(0, half - 1), pl.ds(0, KERNEL + rc)], all_sem.at[4])
    gf_copy(1 - core).wait_recv()
    ggain_ref[...] = gf_v[0, 0:KERNEL] + gf_v[1, 0:KERNEL]
    gcomp_ref[0:hr, :] = gf_v[0, KERNEL : KERNEL + hr]
    gcomp_ref[hr:DH, :] = gf_v[1, KERNEL : KERNEL + hr]
    gf_copy(core).wait_send()


def finish(*refs):
    sources, targets, sem = refs[:5], refs[5:10], refs[10]
    copies = [
        pltpu.make_async_copy(source, target, sem.at[i])
        for i, (source, target) in enumerate(zip(sources, targets))
    ]
    for copy in copies:
        copy.start()
    for copy in copies:
        copy.wait()


def body(n, keys, queries, teacher_map, slab_index, pos_gain, w_comp):
    rows, count = teacher_map.shape
    nb = count // n
    half = n // 2
    gb = rows if count <= 1024 else min(rows, LANES)
    rc = -(-(DH // 2) // half)
    slot_rows = nb - (-(rc + 1) // 8) * 8
    dma = pltpu.SemaphoreType.DMA
    vmem = pl.BlockSpec(memory_space=pltpu.VMEM)
    hbm = pl.BlockSpec(memory_space=pltpu.HBM)
    shapes = (
            jax.ShapeDtypeStruct((1, DH), f32),
            jax.ShapeDtypeStruct((rows, HEADS * DH), bf16),
            jax.ShapeDtypeStruct(keys.shape, bf16),
            jax.ShapeDtypeStruct((DH, DH), f32),
            jax.ShapeDtypeStruct((KERNEL, DH), f32),
        )
    results = pl.pallas_call(
        functools.partial(kernel, n, gb, rc),
        out_shape=shapes,
        in_specs=[pl.BlockSpec(memory_space=pltpu.SMEM)] + [hbm] * 5,
        out_specs=(vmem,) * 5,
        scratch_shapes=[
            pltpu.VMEM(keys.shape, bf16),
            pltpu.VMEM(pos_gain.shape, f32),
            pltpu.VMEM(w_comp.shape, bf16),
            pltpu.VMEM((rows, HEADS * DH), bf16),
            pltpu.VMEM((rows, count), bf16),
            pltpu.VMEM((half, 2, nb + 16, DH), bf16),
            pltpu.VMEM((STRIDE, DH), bf16),
            pltpu.VMEM((count, DH), bf16),
            pltpu.VMEM((count, DH), bf16),
            pltpu.VMEM((DH, count), bf16),
            pltpu.VMEM((count, gb), f32),
            pltpu.VMEM((count, gb), f32),
            pltpu.VMEM((HEADS, count, gb), f32),
            pltpu.VMEM((HEADS, count, gb) if gb == rows else (8, LANES), f32),
            pltpu.VMEM((count, HEADS * gb), bf16),
            pltpu.VMEM((HEADS * gb, DH), bf16),
            pltpu.VMEM((count, gb), f32),
            pltpu.VMEM((count, gb), f32),
            pltpu.VMEM((HEADS, 8, gb), f32),
            pltpu.VMEM((HEADS, 8, gb), f32),
            pltpu.VMEM((2, half, slot_rows, DH), f32),
            pltpu.VMEM((half, slot_rows, DH), f32),
            pltpu.VMEM((half, slot_rows, DH), f32),
            pltpu.VMEM((half, KERNEL + max(rc, 8), DH), f32),
            pltpu.VMEM((2, KERNEL + DH // 2, DH), f32),
            pltpu.VMEM((nb, DH), f32),
            pltpu.VMEM((8, DH), f32),
            dma((6,)),
        ]
        + [dma((count // LANES,))] * 2
        + [dma((6,)), dma((10,))],
        compiler_params=pltpu.CompilerParams(
            collective_id=0, has_side_effects=True, vmem_limit_bytes=(24 if gb == rows else 56) * 1024 * 1024
        ),
    )(slab_index, *[pltpu.with_memory_space_constraint(x, pltpu.HBM) for x in (keys, pos_gain, w_comp, queries, teacher_map)])
    any_space = pl.BlockSpec(memory_space=pl.ANY)
    loss, gq, gk, gcomp, ggain = pl.pallas_call(
        finish,
        out_shape=shapes,
        in_specs=[any_space] * 5,
        out_specs=[any_space] * 5,
        scratch_shapes=[dma((5,))],
        compiler_params=pltpu.CompilerParams(vmem_limit_bytes=4 * 1024 * 1024),
    )(*results)
    return (loss[0, 0:1], gq, gk, gcomp, ggain)


def solution(mesh):
    in_specs = (
        P(("groups", "ctx"), None),
        P(("groups", "ctx"), None),
        P(("groups", "ctx"), None),
        P(("groups", "ctx")),
        P(),
        P(),
    )
    out_specs = (
        P("groups"),
        P(("groups", "ctx"), None),
        P(("groups", "ctx"), None),
        P("groups", None),
        P("groups", None),
    )
    return jax.shard_map(
        functools.partial(body, mesh.shape["ctx"]),
        mesh=mesh, in_specs=in_specs, out_specs=out_specs, check_vma=False,
    )
```

```python
import functools

import jax
import jax.numpy as jnp
from jax import lax
from jax.experimental import pallas as pl
from jax.experimental.pallas import tpu as pltpu
from jax.sharding import PartitionSpec as P

DH = 128
HEADS = 8
KERNEL = 32
STRIDE = 16
LANES = 128
TILE = 16
TILE_UNROLL = 8
HEAD_UNROLL = 8
GQ_UNROLL = 4
CHUNK_UNROLL = 4

big_negative = -1e30
loss_scale = 256.0
f32 = jnp.float32
bf16 = jnp.bfloat16


def split3(x):
    first = x.astype(bf16)
    rest = x - first.astype(f32)
    second = rest.astype(bf16)
    third = (rest - second.astype(f32)).astype(bf16)
    return first, second, third


def stacked(*pieces):
    fill = -sum(piece.shape[0] for piece in pieces) % 16
    if fill:
        pieces += (jnp.zeros((fill, DH), bf16),)
    return jnp.concatenate(pieces, axis=0)


def remote(src, dst, send_sem, recv_sem, device):
    return pltpu.make_async_remote_copy(
        src_ref=src,
        dst_ref=dst,
        send_sem=send_sem,
        recv_sem=recv_sem,
        device_id={"ctx": device},
        device_id_type=pl.DeviceIdType.MESH,
    )


def loop(count, step, start):
    if count <= 4:
        for i in range(count):
            start = step(i, start)
        return start
    return lax.fori_loop(0, count, step, start)


def aligned(i, size):
    return pl.ds(pl.multiple_of(i * size, size), size)


def fold(x, op):
    rows, lanes = x.shape
    return op(x.reshape(rows // 8, 8, lanes), axis=0)


def kernel(
    n, gb, rc,
    slab_ref, keys_hbm, gain_hbm, w_hbm, q_hbm, t_hbm,
    loss_ref, gq_ref, gk_ref, gcomp_ref, ggain_ref,
    keys_ref, gain_ref, w_ref, q_v, t_v, pool_v, halo_v, pooled_v, comp_v, compt_v,
    bias_v, tp_v, s_v, u_v, g_v, qs_v, pk_v, wt_v, lse_v, cv_v, p_v, pair_v, rb_v, rs_v,
    gs_v, gf_v, gp_v, carry_v,
    local_sem, pair_s, pair_r, all_sem, side_sem,
):
    me = lax.axis_index("ctx")
    rows, count = t_v.shape
    nb = count // n
    inv = DH ** (-0.5)
    core = lax.rem(me, 2)
    mine = lax.div(me, 2)
    half = n // 2
    twin = me + 1 - 2 * core
    upper = lax.div(mine, half // 2)
    far = (half - 1) * (1 - upper)
    toward = 2 * upper - 1

    def other_chips(act):
        def step(i, _):
            chip = far + toward * i

            @pl.when(chip != mine)
            def _():
                act(chip)

            return 0

        lax.fori_loop(0, half, step, 0)

    barrier = pltpu.get_barrier_semaphore()

    def signal(device):
        pl.semaphore_signal(
            barrier, inc=1, device_id={"ctx": device}, device_id_type=pl.DeviceIdType.MESH
        )

    def greet(chip):
        signal(2 * chip)
        signal(2 * chip + 1)

    other_chips(greet)
    signal(twin)

    q_copy = pltpu.make_async_copy(q_hbm, q_v, local_sem.at[0])
    t_copy = pltpu.make_async_copy(t_hbm, t_v, local_sem.at[1])
    keys_copy = pltpu.make_async_copy(keys_hbm, keys_ref, local_sem.at[3])
    gain_copy = pltpu.make_async_copy(gain_hbm, gain_ref, local_sem.at[4])
    w_copy = pltpu.make_async_copy(w_hbm, w_ref, local_sem.at[5])
    keys_copy.start()
    gain_copy.start()
    t_copy.start()
    w_copy.start()
    q_copy.start()

    keys_copy.wait()
    gain_copy.wait()
    keys3 = keys_ref[...].astype(f32).reshape(nb, STRIDE, DH)
    gain_lo = gain_ref[0:STRIDE, :]
    gain_hi = gain_ref[STRIDE:KERNEL, :]
    low = jnp.sum(keys3 * gain_lo[None], axis=1)
    high = jnp.sum(keys3 * gain_hi[None], axis=1)
    pool_v[mine, core, 0:nb] = (low + jnp.concatenate([high[1:], high[:1]], axis=0)).astype(bf16)
    pool_v[mine, core, nb : nb + 16] = stacked(*split3(low[nb - 1 : nb]), *split3(high[0:1]))

    @pl.when(me == n - 1)
    def _():
        halo_v[...] = jnp.zeros((STRIDE, DH), bf16)

    @pl.when(me == 0)
    def _():
        carry_v[...] = jnp.zeros((8, DH), f32)

    t_copy.wait()
    place0 = slab_ref[0] * rows

    def prepare(base):
        def first(c, total):
            for l0 in range(0, gb, LANES):
                teach = t_v[pl.ds(base + l0, LANES), aligned(c, LANES)].astype(f32).T
                end = STRIDE * (c * LANES + lax.broadcasted_iota(jnp.int32, (LANES, LANES), 0)) + (KERNEL - 1)
                place = place0 + base + l0 + lax.broadcasted_iota(jnp.int32, (LANES, LANES), 1)
                visible = end <= place
                seen = jnp.where(visible, teach, 0.0)
                bias_v[aligned(c, LANES), l0 : l0 + LANES] = jnp.where(visible, 0.0, big_negative)
                tp_v[aligned(c, LANES), l0 : l0 + LANES] = seen
                part = fold(seen, jnp.sum)
                total = total[:l0 // LANES] + (total[l0 // LANES] + part,) + total[l0 // LANES + 1 :]
            return total

        zero = jnp.zeros((8, LANES), f32)
        total8 = loop(count // LANES, first, (zero,) * (gb // LANES))
        kl8 = zero
        for l0 in range(0, gb, LANES):
            total = jnp.sum(total8[l0 // LANES], axis=0, keepdims=True)
            safe = jnp.where(total > 0, total, 1.0)
            shift = 3.0 - jnp.log2(safe)

            def second(c, acc):
                at = (aligned(c, LANES), slice(l0, l0 + LANES))
                seen = tp_v[at]
                tprob = seen / safe
                tp_v[at] = tprob
                return acc + fold(tprob * (jnp.log2(jnp.maximum(seen, 1e-30)) + shift), jnp.sum)

            kl8 = loop(count // LANES, second, kl8)
        return kl8

    def stack(base):
        for h in range(HEADS):
            qs_v[h * gb : (h + 1) * gb, :] = q_v[pl.ds(base, gb), h * DH : (h + 1) * DH]

    whole = gb == rows
    e_v = u_v if whole else s_v
    kl_start = prepare(0) if whole else jnp.zeros((8, LANES), f32)

    pl.semaphore_wait(barrier, n - 1)

    def pool_copy(chip):
        block = pool_v.at[mine, core]
        return remote(block, block, all_sem.at[0], all_sem.at[1], 2 * chip + core)

    def relay_copy(c):
        blocks = pool_v.at[:, c]
        return remote(blocks, blocks, side_sem.at[8], side_sem.at[9], twin)

    def wait_bytes(ref, sem):
        pltpu.make_async_copy(ref, ref, sem).wait()

    other_chips(lambda chip: pool_copy(chip).start())

    def halo_copy(dst):
        return remote(
            keys_ref.at[pl.ds(0, STRIDE)], halo_v, side_sem.at[0], side_sem.at[1], dst
        )

    @pl.when(me > 0)
    def _():
        halo_copy(me - 1).start()

    w_copy.wait()
    q_copy.wait()
    if whole:
        stack(0)
    wait_bytes(pool_v.at[pl.ds(0, half - 1), 0], all_sem.at[1])
    relay_copy(core).start()
    relay_copy(1 - core).wait_recv()
    blocks = pool_v[...].reshape(n, nb + 16, DH)
    last_row = lax.broadcasted_iota(jnp.int32, (n, nb, DH), 1) == nb - 1
    ends = blocks[:, nb : nb + 16, :].astype(f32)
    low_end = (ends[:, 2:3] + ends[:, 1:2]) + ends[:, 0:1]
    high_end = (ends[:, 5:6] + ends[:, 4:5]) + ends[:, 3:4]
    edges = low_end + jnp.concatenate(
        [high_end[1:], jnp.zeros((1, 1, DH), f32)], axis=0
    )
    pooled = jnp.where(last_row, edges, blocks[:, 0:nb, :].astype(f32)).astype(bf16)
    pooled_v[...] = pooled.reshape(count, DH)
    comp_v[...] = jnp.dot(
        pooled_v[...], w_ref[...], preferred_element_type=f32
    ).astype(bf16)

    nt = (((1,), (1,)), ((), ()))
    tn = (((0,), (0,)), ((), ()))
    to_log2 = inv * 1.4426950408889634

    def probabilities(base, kl8):
        queries_at = pl.ds(base, gb)

        def head(h, _):
            qh = q_v[queries_at, aligned(h, DH)]

            def scores(c, top):
                s = lax.dot_general(
                    comp_v[aligned(c, LANES), :], qh, nt, preferred_element_type=f32
                )
                s = s * to_log2 + bias_v[aligned(c, LANES), :]
                s_v[h, aligned(c, LANES), :] = s
                return jnp.maximum(top, fold(s, jnp.max))

            top8 = loop(count // LANES, scores, jnp.full((8, gb), 2 * big_negative, f32))
            top = jnp.max(top8, axis=0, keepdims=True)

            def sums(c, total):
                return total + fold(jnp.exp2(s_v[h, aligned(c, LANES), :] - top), jnp.sum)

            total8 = loop(count // LANES, sums, jnp.zeros((8, gb), f32))
            total = jnp.sum(total8, axis=0, keepdims=True)
            lse = jnp.where(top > 0.5 * big_negative, top + jnp.log2(total), 0.0)
            lse_v[h] = jnp.broadcast_to(lse, (8, gb))
            return 0

        lax.fori_loop(0, HEADS, head, 0, unroll=HEAD_UNROLL)

        for l0 in range(0, gb, LANES):
            lanes = slice(l0, l0 + LANES)
            lse = [lse_v[h, :, lanes][None] for h in range(HEADS)]

            def ratios(c, carry):
                kl8, cv = carry
                at = aligned(c, TILE)
                x = []
                for h in range(HEADS):
                    x.append((s_v[h, at, lanes].reshape(TILE // 8, 8, LANES) - lse[h]))
                tops = x
                while len(tops) > 1:
                    tops = [jnp.maximum(a, b) for a, b in zip(tops[::2], tops[1::2])]
                peak = tops[0]
                u = [jnp.exp2(a - peak) for a in x]
                mass = u
                while len(mass) > 1:
                    mass = [a + b for a, b in zip(mass[::2], mass[1::2])]
                mass = mass[0]
                tprob = tp_v[at, lanes].reshape(TILE // 8, 8, LANES)
                weight = tprob / mass
                kl8 = kl8 - jnp.sum(tprob * (peak + jnp.log2(mass)), axis=0)
                pk_v[at, lanes] = jnp.exp2(peak).reshape(TILE, LANES)
                wt_v[at, lanes] = (loss_scale * weight).reshape(TILE, LANES)
                for h in range(HEADS):
                    e_v[h, at, lanes] = u[h].reshape(TILE, LANES)
                cv = tuple(a + jnp.sum(b * weight, axis=0) for a, b in zip(cv, u))
                return kl8, cv

            zero = jnp.zeros((8, LANES), f32)
            kl8, cv = lax.fori_loop(
                0, count // TILE, ratios, (kl8, (zero,) * HEADS), unroll=TILE_UNROLL
            )
            for h in range(HEADS):
                total = loss_scale * jnp.sum(cv[h], axis=0, keepdims=True)
                cv_v[h, :, lanes] = jnp.broadcast_to(total, (8, LANES))
        return kl8

    def block_grads(base, i, first, comp_part):
        c = first_chunk + chunk_step * i
        at = aligned(c, LANES)
        peak = pk_v[at, :].reshape(LANES // 8, 8, gb)
        weight = wt_v[at, :].reshape(LANES // 8, 8, gb)
        for h in range(HEADS):
            u = e_v[h, at, :].reshape(LANES // 8, 8, gb)
            g = u * (peak * cv_v[h][None] - weight)
            g_v[at, h * gb : (h + 1) * gb] = g.reshape(LANES, gb).astype(bf16)
        acc = jnp.dot(g_v[at, :], qs_v[...], preferred_element_type=f32)
        acc = acc * inv
        for k in range(LANES // nb):
            where = (k % 2, c * (LANES // nb // 2) + k // 2)
            if first:
                p_v[where + (slice(0, nb),)] = acc[k * nb : (k + 1) * nb]
            else:
                p_v[where + (slice(0, nb),)] += acc[k * nb : (k + 1) * nb]
        pieces = split3(acc)
        block = pooled_v[aligned(c, LANES), :]
        add = lax.dot_general(
            jnp.concatenate([block] * 3, axis=0),
            jnp.concatenate(pieces[::-1], axis=0),
            tn,
            preferred_element_type=f32,
        )
        return c, comp_part + add

    def query_grads(base, h0, h1):
        def head(h, _):
            gq = jnp.dot(compt_v[...], g_v[:, aligned(h, gb)], preferred_element_type=f32) * inv
            gq_ref[pl.ds(base, gb), aligned(h, DH)] = gq.T.astype(bf16)
            return 0

        lax.fori_loop(h0, h1, head, 0, unroll=GQ_UNROLL)

    used = nb + rc + 1

    def pair_copy(c):
        at = (pl.ds(c * per_chunk, per_chunk), pl.ds(0, nb))
        return remote(
            p_v.at[(1 - core,) + at], pair_v.at[at], pair_s.at[c], pair_r.at[c], twin
        )

    def side_copy():
        at = (slice(None), pl.ds(nb, rc + 1))
        return remote(
            p_v.at[(1 - core,) + at], pair_v.at[at], side_sem.at[4], side_sem.at[5], twin
        )

    def rs_copy(dst):
        return remote(
            rb_v.at[dst], rs_v.at[mine], all_sem.at[2], all_sem.at[3], 2 * dst + core
        )

    chunks = count // LANES
    per_chunk = LANES // nb // 2
    first_chunk = (chunks - 1) * (1 - upper)
    chunk_step = toward

    no_part = jnp.zeros((DH, DH), f32)
    if whole:
        kl8 = probabilities(0, kl_start)

        def chunk(i, part):
            c, part = block_grads(0, i, True, part)
            pair_copy(c).start()
            return part

        comp_part = lax.fori_loop(0, chunks, chunk, no_part, unroll=CHUNK_UNROLL)
    else:
        compt_v[...] = comp_v[...].astype(f32).T.astype(bf16)
        p_v[...] = jnp.zeros_like(p_v)

        def group(i, carry):
            kl8, part = carry
            base = pl.multiple_of(i * gb, gb)
            stack(base)
            kl8 = probabilities(base, kl8 + prepare(base))
            part = lax.fori_loop(0, chunks, lambda k, a: block_grads(base, k, False, a)[1], part)
            query_grads(base, 0, HEADS)
            return kl8, part

        kl8, comp_part = lax.fori_loop(0, rows // gb, group, (kl_start, no_part))

        def send_pair(c, _):
            pair_copy(c).start()
            return 0

        lax.fori_loop(0, chunks, send_pair, 0)

    kl_total = jnp.sum(jnp.sum(kl8, axis=0, keepdims=True), axis=1, keepdims=True)
    kl_row = jnp.broadcast_to(kl_total * 0.6931471805599453, (1, DH))
    hr = DH // 2
    for c in range(2):
        for d in range(half):
            if (d + 1) * rc <= hr:
                p_v[c, d, nb : nb + rc] = comp_part[c * hr + d * rc : c * hr + (d + 1) * rc]
            else:
                p_v[c, d, nb : nb + rc] = jnp.zeros((rc, DH), f32)
            p_v[c, d, nb + rc : used] = kl_row

    side_copy().start()
    if whole:
        compt_v[...] = comp_v[...].astype(f32).T.astype(bf16)

    def forward(i, _):
        c = first_chunk + chunk_step * i
        pair_copy(c).wait_recv()

        @pl.when(i == 0)
        def _():
            side_copy().wait_recv()

        for k in range(per_chunk):
            chip = c * per_chunk + k
            total = p_v[core, chip, 0:used] + pair_v[chip, 0:used]
            message = (total[0:nb].astype(bf16), stacked(total[nb : nb + rc].astype(bf16), *split3(total[nb + rc :])))

            @pl.when(chip != mine)
            def _():
                rb_v[chip, 0:nb] = message[0]
                rb_v[chip, nb:] = message[1]
                rs_copy(chip).start()

            @pl.when(chip == mine)
            def _():
                rs_v[mine, 0:nb] = message[0]
                rs_v[mine, nb:] = message[1]

        return 0

    lax.fori_loop(0, chunks, forward, 0)
    if whole:
        query_grads(0, 0, HEADS)

    @pl.when(me < n - 1)
    def _():
        halo_copy(me).wait_recv()

    upper3 = jnp.concatenate(
        [keys3[1:], halo_v[...].astype(f32).reshape(1, STRIDE, DH)], axis=0
    )

    wait_bytes(rs_v.at[pl.ds(0, half - 1)], all_sem.at[3])
    sums = lax.fori_loop(
        1, half, lambda d, total: total + rs_v[d].astype(f32), rs_v[0].astype(f32)
    )
    own = sums[0:nb]
    own3 = split3(own)
    gp3 = lax.dot_general(
        jnp.concatenate(own3, axis=0), w_ref[...], nt, preferred_element_type=f32
    )
    grad_pooled = (gp3[2 * nb :] + gp3[nb : 2 * nb]) + gp3[:nb]
    gp_v[...] = grad_pooled

    def carry_copy(dst):
        return remote(
            gp_v.at[pl.ds(nb - 8, 8)], carry_v, side_sem.at[2], side_sem.at[3], dst
        )

    gs_v[mine, 0:STRIDE] = jnp.sum(grad_pooled[:, None, :] * keys3, axis=0).astype(bf16)
    gs_v[mine, STRIDE:KERNEL] = jnp.sum(grad_pooled[:, None, :] * upper3, axis=0).astype(bf16)
    gs_v[mine, KERNEL:] = stacked(*split3(sums[nb : nb + rc])[0:2])
    last = nb + rc
    kl_sum = (sums[last + 2 : last + 3] + sums[last + 1 : last + 2]) + sums[last : last + 1]
    loss_ref[...] = kl_sum * (1.0 / (rows * n))

    def gs_copy(dst):
        piece = gs_v.at[mine]
        return remote(piece, piece, all_sem.at[4], all_sem.at[5], 2 * dst + core)

    other_chips(lambda chip: gs_copy(chip).start())

    @pl.when(me < n - 1)
    def _():
        carry_copy(me + 1).start()

    @pl.when(me > 0)
    def _():
        carry_copy(me).wait_recv()

    before = jnp.concatenate([carry_v[7:8, :], grad_pooled[: nb - 1]], axis=0)
    grad_keys = grad_pooled[:, None, :] * gain_lo[None] + before[:, None, :] * gain_hi[None]
    gk_ref[...] = grad_keys.reshape(nb * STRIDE, DH).astype(bf16)

    wait_bytes(pool_v.at[pl.ds(0, half - 1), 0], all_sem.at[0])
    relay_copy(core).wait_send()
    wait_bytes(rs_v.at[pl.ds(0, half - 1)], all_sem.at[2])

    def drop_pair(c, _):
        pair_copy(c).wait_send()
        return 0

    lax.fori_loop(0, chunks, drop_pair, 0)
    side_copy().wait_send()

    @pl.when(me > 0)
    def _():
        halo_copy(me - 1).wait_send()

    @pl.when(me < n - 1)
    def _():
        carry_copy(me + 1).wait_send()

    wait_bytes(gs_v.at[pl.ds(0, half - 1)], all_sem.at[5])
    gf_v[core, 0:KERNEL] = lax.fori_loop(
        1, half,
        lambda d, total: total + gs_v[d, 0:KERNEL].astype(f32),
        gs_v[0, 0:KERNEL].astype(f32),
    )
    for d in range(half):
        if (d + 1) * rc <= hr:
            piece = gs_v[d, KERNEL:].astype(f32)
            gf_v[core, KERNEL + d * rc : KERNEL + (d + 1) * rc] = piece[0:rc] + piece[rc : 2 * rc]

    def gf_copy(slot):
        return remote(gf_v.at[slot], gf_v.at[slot], side_sem.at[6], side_sem.at[7], twin)

    gf_copy(core).start()
    wait_bytes(gs_v.at[pl.ds(0, half - 1)], all_sem.at[4])
    gf_copy(1 - core).wait_recv()
    ggain_ref[...] = gf_v[0, 0:KERNEL] + gf_v[1, 0:KERNEL]
    gcomp_ref[0:hr, :] = gf_v[0, KERNEL : KERNEL + hr]
    gcomp_ref[hr:DH, :] = gf_v[1, KERNEL : KERNEL + hr]
    gf_copy(core).wait_send()


def finish(*refs):
    sources, targets, sem = refs[:5], refs[5:10], refs[10]
    copies = [
        pltpu.make_async_copy(source, target, sem.at[i])
        for i, (source, target) in enumerate(zip(sources, targets))
    ]
    for copy in copies:
        copy.start()
    for copy in copies:
        copy.wait()


def body(n, keys, queries, teacher_map, slab_index, pos_gain, w_comp):
    rows, count = teacher_map.shape
    nb = count // n
    half = n // 2
    gb = rows if count <= 1024 else min(rows, LANES)
    rc = -(-(DH // 2) // half)
    slot_rows = nb - (-(rc + 1) // 8) * 8
    dma = pltpu.SemaphoreType.DMA
    vmem = pl.BlockSpec(memory_space=pltpu.VMEM)
    hbm = pl.BlockSpec(memory_space=pltpu.HBM)
    shapes = (
            jax.ShapeDtypeStruct((1, DH), f32),
            jax.ShapeDtypeStruct((rows, HEADS * DH), bf16),
            jax.ShapeDtypeStruct(keys.shape, bf16),
            jax.ShapeDtypeStruct((DH, DH), f32),
            jax.ShapeDtypeStruct((KERNEL, DH), f32),
        )
    results = pl.pallas_call(
        functools.partial(kernel, n, gb, rc),
        out_shape=shapes,
        in_specs=[pl.BlockSpec(memory_space=pltpu.SMEM)] + [hbm] * 5,
        out_specs=(vmem,) * 5,
        scratch_shapes=[
            pltpu.VMEM(keys.shape, bf16),
            pltpu.VMEM(pos_gain.shape, f32),
            pltpu.VMEM(w_comp.shape, bf16),
            pltpu.VMEM((rows, HEADS * DH), bf16),
            pltpu.VMEM((rows, count), bf16),
            pltpu.VMEM((half, 2, nb + 16, DH), bf16),
            pltpu.VMEM((STRIDE, DH), bf16),
            pltpu.VMEM((count, DH), bf16),
            pltpu.VMEM((count, DH), bf16),
            pltpu.VMEM((DH, count), bf16),
            pltpu.VMEM((count, gb), f32),
            pltpu.VMEM((count, gb), f32),
            pltpu.VMEM((HEADS, count, gb), f32),
            pltpu.VMEM((HEADS, count, gb) if gb == rows else (8, LANES), f32),
            pltpu.VMEM((count, HEADS * gb), bf16),
            pltpu.VMEM((HEADS * gb, DH), bf16),
            pltpu.VMEM((count, gb), f32),
            pltpu.VMEM((count, gb), f32),
            pltpu.VMEM((HEADS, 8, gb), f32),
            pltpu.VMEM((HEADS, 8, gb), f32),
            pltpu.VMEM((2, half, slot_rows, DH), f32),
            pltpu.VMEM((half, slot_rows, DH), f32),
            pltpu.VMEM((half, nb - (-(rc + 3) // 16) * 16, DH), bf16),
            pltpu.VMEM((half, nb - (-(rc + 3) // 16) * 16, DH), bf16),
            pltpu.VMEM((half, KERNEL - (-2 * rc // 16) * 16, DH), bf16),
            pltpu.VMEM((2, KERNEL + DH // 2, DH), f32),
            pltpu.VMEM((nb, DH), f32),
            pltpu.VMEM((8, DH), f32),
            dma((6,)),
        ]
        + [dma((count // LANES,))] * 2
        + [dma((6,)), dma((10,))],
        compiler_params=pltpu.CompilerParams(
            collective_id=0, has_side_effects=True, vmem_limit_bytes=(24 if gb == rows else 56) * 1024 * 1024
        ),
    )(slab_index, *[pltpu.with_memory_space_constraint(x, pltpu.HBM) for x in (keys, pos_gain, w_comp, queries, teacher_map)])
    any_space = pl.BlockSpec(memory_space=pl.ANY)
    loss, gq, gk, gcomp, ggain = pl.pallas_call(
        finish,
        out_shape=shapes,
        in_specs=[any_space] * 5,
        out_specs=[any_space] * 5,
        scratch_shapes=[dma((5,))],
        compiler_params=pltpu.CompilerParams(vmem_limit_bytes=4 * 1024 * 1024),
    )(*results)
    return (loss[0, 0:1], gq, gk, gcomp, ggain)


def solution(mesh):
    in_specs = (
        P(("groups", "ctx"), None),
        P(("groups", "ctx"), None),
        P(("groups", "ctx"), None),
        P(("groups", "ctx")),
        P(),
        P(),
    )
    out_specs = (
        P("groups"),
        P(("groups", "ctx"), None),
        P(("groups", "ctx"), None),
        P("groups", None),
        P("groups", None),
    )
    return jax.shard_map(
        functools.partial(body, mesh.shape["ctx"]),
        mesh=mesh, in_specs=in_specs, out_specs=out_specs, check_vma=False,
    )
```

```python
import functools

import jax
import jax.numpy as jnp
from jax import lax
from jax.experimental import pallas as pl
from jax.experimental.pallas import tpu as pltpu
from jax.sharding import PartitionSpec as P

DH = 128
HEADS = 8
KERNEL = 32
STRIDE = 16
LANES = 128
TILE = 16
TILE_UNROLL = 8
HEAD_UNROLL = 8
GQ_UNROLL = 4
CHUNK_UNROLL = 4

big_negative = -1e30
loss_scale = 256.0
f32 = jnp.float32
bf16 = jnp.bfloat16


def split3(x):
    first = x.astype(bf16)
    rest = x - first.astype(f32)
    second = rest.astype(bf16)
    third = (rest - second.astype(f32)).astype(bf16)
    return first, second, third


def stacked(*pieces):
    fill = -sum(piece.shape[0] for piece in pieces) % 16
    if fill:
        pieces += (jnp.zeros((fill, DH), bf16),)
    return jnp.concatenate(pieces, axis=0)


def remote(src, dst, send_sem, recv_sem, device):
    return pltpu.make_async_remote_copy(
        src_ref=src,
        dst_ref=dst,
        send_sem=send_sem,
        recv_sem=recv_sem,
        device_id={"ctx": device},
        device_id_type=pl.DeviceIdType.MESH,
    )


def loop(count, step, start):
    if count <= 8:
        for i in range(count):
            start = step(i, start)
        return start
    return lax.fori_loop(0, count, step, start)


def aligned(i, size):
    return pl.ds(pl.multiple_of(i * size, size), size)


def fold(x, op):
    rows, lanes = x.shape
    return op(x.reshape(rows // 8, 8, lanes), axis=0)


def kernel(
    n, gb, rc,
    slab_ref, keys_hbm, gain_hbm, w_hbm, q_hbm, t_hbm,
    loss_ref, gq_ref, gk_ref, gcomp_ref, ggain_ref,
    keys_ref, gain_ref, w_ref, q_v, t_v, pool_v, edge_v, halo_v, pooled_v, comp_v, compt_v,
    bias_v, tp_v, s_v, u_v, g_v, qs_v, pk_v, wt_v, lse_v, cv_v, p_v, pair_v, rb_v, rs_v,
    gs_v, gf_v, gp_v, carry_v,
    local_sem, pair_s, pair_r, all_sem, side_sem,
):
    me = lax.axis_index("ctx")
    rows, count = t_v.shape
    nb = count // n
    inv = DH ** (-0.5)
    core = lax.rem(me, 2)
    mine = lax.div(me, 2)
    half = n // 2
    twin = me + 1 - 2 * core
    upper = lax.div(mine, half // 2)
    far = (half - 1) * (1 - upper)
    toward = 2 * upper - 1

    def other_chips(act):
        def step(i, _):
            chip = far + toward * i

            @pl.when(chip != mine)
            def _():
                act(chip)

            return 0

        lax.fori_loop(0, half, step, 0)

    barrier = pltpu.get_barrier_semaphore()

    def signal(device):
        pl.semaphore_signal(
            barrier, inc=1, device_id={"ctx": device}, device_id_type=pl.DeviceIdType.MESH
        )

    def greet(chip):
        signal(2 * chip)
        signal(2 * chip + 1)

    other_chips(greet)
    signal(twin)

    q_copy = pltpu.make_async_copy(q_hbm, q_v, local_sem.at[0])
    t_copy = pltpu.make_async_copy(t_hbm, t_v, local_sem.at[1])
    keys_copy = pltpu.make_async_copy(keys_hbm, keys_ref, local_sem.at[3])
    gain_copy = pltpu.make_async_copy(gain_hbm, gain_ref, local_sem.at[4])
    w_copy = pltpu.make_async_copy(w_hbm, w_ref, local_sem.at[5])
    keys_copy.start()
    gain_copy.start()
    t_copy.start()
    w_copy.start()
    q_copy.start()

    keys_copy.wait()
    gain_copy.wait()
    keys3 = keys_ref[...].astype(f32).reshape(nb, STRIDE, DH)
    gain_lo = gain_ref[0:STRIDE, :]
    gain_hi = gain_ref[STRIDE:KERNEL, :]
    low = jnp.sum(keys3 * gain_lo[None], axis=1)
    high = jnp.sum(keys3 * gain_hi[None], axis=1)
    pool_v[mine, core] = (low + jnp.concatenate([high[1:], high[:1]], axis=0)).astype(bf16)
    edge_v[mine, core, 0:1] = low[nb - 1 : nb]
    edge_v[mine, core, 1:2] = high[0:1]

    @pl.when(me == n - 1)
    def _():
        halo_v[...] = jnp.zeros((STRIDE, DH), bf16)

    @pl.when(me == 0)
    def _():
        carry_v[...] = jnp.zeros((8, DH), f32)

    place0 = slab_ref[0] * rows

    def prepare(base):
        def first(c, total):
            for l0 in range(0, gb, LANES):
                teach = t_v[pl.ds(base + l0, LANES), aligned(c, LANES)].astype(f32).T
                end = STRIDE * (c * LANES + lax.broadcasted_iota(jnp.int32, (LANES, LANES), 0)) + (KERNEL - 1)
                place = place0 + base + l0 + lax.broadcasted_iota(jnp.int32, (LANES, LANES), 1)
                visible = end <= place
                seen = jnp.where(visible, teach, 0.0)
                bias_v[aligned(c, LANES), l0 : l0 + LANES] = jnp.where(visible, 0.0, big_negative)
                tp_v[aligned(c, LANES), l0 : l0 + LANES] = seen
                part = fold(seen, jnp.sum)
                total = total[:l0 // LANES] + (total[l0 // LANES] + part,) + total[l0 // LANES + 1 :]
            return total

        zero = jnp.zeros((8, LANES), f32)
        total8 = loop(count // LANES, first, (zero,) * (gb // LANES))
        kl8 = zero
        for l0 in range(0, gb, LANES):
            total = jnp.sum(total8[l0 // LANES], axis=0, keepdims=True)
            safe = jnp.where(total > 0, total, 1.0)
            shift = 3.0 - jnp.log2(safe)

            def second(c, acc):
                at = (aligned(c, LANES), slice(l0, l0 + LANES))
                seen = tp_v[at]
                tprob = seen / safe
                tp_v[at] = tprob
                return acc + fold(tprob * (jnp.log2(jnp.maximum(seen, 1e-30)) + shift), jnp.sum)

            kl8 = loop(count // LANES, second, kl8)
        return kl8

    def stack(base):
        for h in range(HEADS):
            qs_v[h * gb : (h + 1) * gb, :] = q_v[pl.ds(base, gb), h * DH : (h + 1) * DH]

    whole = gb == rows
    e_v = u_v if whole else s_v
    pl.semaphore_wait(barrier, n - 1)

    def pool_copy(chip):
        block = pool_v.at[mine, core]
        return remote(block, block, all_sem.at[0], all_sem.at[1], 2 * chip + core)

    def edge_copy(chip):
        ends = edge_v.at[mine, core, pl.ds(0, 2)]
        return remote(ends, ends, all_sem.at[6], all_sem.at[7], 2 * chip + core)

    def relay_copy(c):
        blocks = pool_v.at[:, c]
        return remote(blocks, blocks, side_sem.at[8], side_sem.at[9], twin)

    def relay_edges(c):
        ends = edge_v.at[:, c, pl.ds(0, 2)]
        return remote(ends, ends, all_sem.at[8], all_sem.at[9], twin)

    def wait_bytes(ref, sem):
        pltpu.make_async_copy(ref, ref, sem).wait()

    other_chips(lambda chip: pool_copy(chip).start())
    other_chips(lambda chip: edge_copy(chip).start())

    def halo_copy(dst):
        return remote(
            keys_ref.at[pl.ds(0, STRIDE)], halo_v, side_sem.at[0], side_sem.at[1], dst
        )

    @pl.when(me > 0)
    def _():
        halo_copy(me - 1).start()

    t_copy.wait()
    kl_start = prepare(0) if whole else jnp.zeros((8, LANES), f32)
    w_copy.wait()
    q_copy.wait()
    if whole:
        stack(0)
    wait_bytes(pool_v.at[pl.ds(0, half - 1), 0], all_sem.at[1])
    relay_copy(core).start()
    wait_bytes(edge_v.at[pl.ds(0, half - 1), 0, pl.ds(0, 2)], all_sem.at[7])
    relay_edges(core).start()
    relay_copy(1 - core).wait_recv()
    relay_edges(1 - core).wait_recv()
    blocks = pool_v[...].reshape(n, nb, DH)
    last_row = lax.broadcasted_iota(jnp.int32, (n, nb, DH), 1) == nb - 1
    ends = edge_v[...].reshape(n, 8, DH)
    edges = ends[:, 0:1] + jnp.concatenate(
        [ends[1:, 1:2], jnp.zeros((1, 1, DH), f32)], axis=0
    )
    pooled = jnp.where(last_row, edges, blocks.astype(f32)).astype(bf16)
    pooled_v[...] = pooled.reshape(count, DH)
    comp_v[...] = jnp.dot(
        pooled_v[...], w_ref[...], preferred_element_type=f32
    ).astype(bf16)

    nt = (((1,), (1,)), ((), ()))
    tn = (((0,), (0,)), ((), ()))
    to_log2 = inv * 1.4426950408889634

    def probabilities(base, kl8):
        queries_at = pl.ds(base, gb)

        def head(h, _):
            qh = q_v[queries_at, aligned(h, DH)]

            def scores(c, top):
                s = lax.dot_general(
                    comp_v[aligned(c, LANES), :], qh, nt, preferred_element_type=f32
                )
                s = s * to_log2 + bias_v[aligned(c, LANES), :]
                s_v[h, aligned(c, LANES), :] = s
                return jnp.maximum(top, fold(s, jnp.max))

            top8 = loop(count // LANES, scores, jnp.full((8, gb), 2 * big_negative, f32))
            top = jnp.max(top8, axis=0, keepdims=True)

            def sums(c, total):
                return total + fold(jnp.exp2(s_v[h, aligned(c, LANES), :] - top), jnp.sum)

            total8 = loop(count // LANES, sums, jnp.zeros((8, gb), f32))
            total = jnp.sum(total8, axis=0, keepdims=True)
            lse = jnp.where(top > 0.5 * big_negative, top + jnp.log2(total), 0.0)
            lse_v[h] = jnp.broadcast_to(lse, (8, gb))
            return 0

        lax.fori_loop(0, HEADS, head, 0, unroll=HEAD_UNROLL)

        for l0 in range(0, gb, LANES):
            lanes = slice(l0, l0 + LANES)
            lse = [lse_v[h, :, lanes][None] for h in range(HEADS)]

            def ratios(c, carry):
                kl8, cv = carry
                at = aligned(c, TILE)
                x = []
                for h in range(HEADS):
                    x.append((s_v[h, at, lanes].reshape(TILE // 8, 8, LANES) - lse[h]))
                tops = x
                while len(tops) > 1:
                    tops = [jnp.maximum(a, b) for a, b in zip(tops[::2], tops[1::2])]
                peak = tops[0]
                u = [jnp.exp2(a - peak) for a in x]
                mass = u
                while len(mass) > 1:
                    mass = [a + b for a, b in zip(mass[::2], mass[1::2])]
                mass = mass[0]
                tprob = tp_v[at, lanes].reshape(TILE // 8, 8, LANES)
                weight = tprob / mass
                kl8 = kl8 - jnp.sum(tprob * (peak + jnp.log2(mass)), axis=0)
                pk_v[at, lanes] = jnp.exp2(peak).reshape(TILE, LANES)
                wt_v[at, lanes] = (loss_scale * weight).reshape(TILE, LANES)
                for h in range(HEADS):
                    e_v[h, at, lanes] = u[h].reshape(TILE, LANES)
                cv = tuple(a + jnp.sum(b * weight, axis=0) for a, b in zip(cv, u))
                return kl8, cv

            zero = jnp.zeros((8, LANES), f32)
            kl8, cv = lax.fori_loop(
                0, count // TILE, ratios, (kl8, (zero,) * HEADS), unroll=TILE_UNROLL
            )
            for h in range(HEADS):
                total = loss_scale * jnp.sum(cv[h], axis=0, keepdims=True)
                cv_v[h, :, lanes] = jnp.broadcast_to(total, (8, LANES))
        return kl8

    def block_grads(base, i, first, comp_part):
        c = first_chunk + chunk_step * i
        at = aligned(c, LANES)
        peak = pk_v[at, :].reshape(LANES // 8, 8, gb)
        weight = wt_v[at, :].reshape(LANES // 8, 8, gb)
        for h in range(HEADS):
            u = e_v[h, at, :].reshape(LANES // 8, 8, gb)
            g = u * (peak * cv_v[h][None] - weight)
            g_v[at, h * gb : (h + 1) * gb] = g.reshape(LANES, gb).astype(bf16)
        acc = jnp.dot(g_v[at, :], qs_v[...], preferred_element_type=f32)
        acc = acc * inv
        for k in range(LANES // nb):
            where = (k % 2, c * (LANES // nb // 2) + k // 2)
            if first:
                p_v[where + (slice(0, nb),)] = acc[k * nb : (k + 1) * nb]
            else:
                p_v[where + (slice(0, nb),)] += acc[k * nb : (k + 1) * nb]
        pieces = split3(acc)
        block = pooled_v[aligned(c, LANES), :]
        add = lax.dot_general(
            jnp.concatenate([block] * 3, axis=0),
            jnp.concatenate(pieces[::-1], axis=0),
            tn,
            preferred_element_type=f32,
        )
        return c, comp_part + add

    def query_grads(base, h0, h1):
        def head(h, _):
            gq = jnp.dot(compt_v[...], g_v[:, aligned(h, gb)], preferred_element_type=f32) * inv
            gq_ref[pl.ds(base, gb), aligned(h, DH)] = gq.T.astype(bf16)
            return 0

        lax.fori_loop(h0, h1, head, 0, unroll=GQ_UNROLL)

    used = nb + rc + 1

    def pair_copy(c):
        at = (pl.ds(c * per_chunk, per_chunk), pl.ds(0, nb))
        return remote(
            p_v.at[(1 - core,) + at], pair_v.at[at], pair_s.at[c], pair_r.at[c], twin
        )

    def side_copy():
        at = (slice(None), pl.ds(nb, rc + 1))
        return remote(
            p_v.at[(1 - core,) + at], pair_v.at[at], side_sem.at[4], side_sem.at[5], twin
        )

    def rs_copy(dst):
        return remote(
            rb_v.at[dst], rs_v.at[mine], all_sem.at[2], all_sem.at[3], 2 * dst + core
        )

    chunks = count // LANES
    per_chunk = LANES // nb // 2
    first_chunk = (chunks - 1) * (1 - upper)
    chunk_step = toward

    no_part = jnp.zeros((DH, DH), f32)
    if whole:
        kl8 = probabilities(0, kl_start)

        def chunk(i, part):
            c, part = block_grads(0, i, True, part)
            pair_copy(c).start()
            return part

        comp_part = lax.fori_loop(0, chunks, chunk, no_part, unroll=CHUNK_UNROLL)
    else:
        compt_v[...] = comp_v[...].astype(f32).T.astype(bf16)
        p_v[...] = jnp.zeros_like(p_v)

        def group(i, carry):
            kl8, part = carry
            base = pl.multiple_of(i * gb, gb)
            stack(base)
            kl8 = probabilities(base, kl8 + prepare(base))
            part = lax.fori_loop(0, chunks, lambda k, a: block_grads(base, k, False, a)[1], part)
            query_grads(base, 0, HEADS)
            return kl8, part

        kl8, comp_part = lax.fori_loop(0, rows // gb, group, (kl_start, no_part))

        def send_pair(c, _):
            pair_copy(c).start()
            return 0

        lax.fori_loop(0, chunks, send_pair, 0)

    kl_total = jnp.sum(jnp.sum(kl8, axis=0, keepdims=True), axis=1, keepdims=True)
    kl_row = jnp.broadcast_to(kl_total * 0.6931471805599453, (1, DH))
    hr = DH // 2
    for c in range(2):
        for d in range(half):
            if (d + 1) * rc <= hr:
                p_v[c, d, nb : nb + rc] = comp_part[c * hr + d * rc : c * hr + (d + 1) * rc]
            else:
                p_v[c, d, nb : nb + rc] = jnp.zeros((rc, DH), f32)
            p_v[c, d, nb + rc : used] = kl_row

    side_copy().start()
    if whole:
        compt_v[...] = comp_v[...].astype(f32).T.astype(bf16)

    side_copy().wait_recv()

    def forward(i, _):
        c = first_chunk + chunk_step * i
        pair_copy(c).wait_recv()
        chips = pl.ds(c * per_chunk, per_chunk)
        total = p_v[core, chips, 0:used] + pair_v[chips, 0:used]
        rb_v[chips, 0:nb] = total[:, 0:nb].astype(bf16)
        for k in range(per_chunk):
            rb_v[c * per_chunk + k, nb:] = stacked(
                total[k, nb : nb + rc].astype(bf16), *split3(total[k, nb + rc :])
            )
        for k in range(per_chunk):
            chip = c * per_chunk + k

            @pl.when(chip != mine)
            def _():
                rs_copy(chip).start()

        return 0

    loop(chunks, forward, 0)
    rs_v[mine] = rb_v[mine]
    if whole:
        query_grads(0, 0, HEADS)

    @pl.when(me < n - 1)
    def _():
        halo_copy(me).wait_recv()

    upper3 = jnp.concatenate(
        [keys3[1:], halo_v[...].astype(f32).reshape(1, STRIDE, DH)], axis=0
    )

    wait_bytes(rs_v.at[pl.ds(0, half - 1)], all_sem.at[3])
    sums = loop(half - 1, lambda d, total: total + rs_v[d + 1].astype(f32), rs_v[0].astype(f32))
    own = sums[0:nb]
    own3 = split3(own)
    gp3 = lax.dot_general(
        jnp.concatenate(own3, axis=0), w_ref[...], nt, preferred_element_type=f32
    )
    grad_pooled = (gp3[2 * nb :] + gp3[nb : 2 * nb]) + gp3[:nb]
    gp_v[...] = grad_pooled

    def carry_copy(dst):
        return remote(
            gp_v.at[pl.ds(nb - 8, 8)], carry_v, side_sem.at[2], side_sem.at[3], dst
        )

    gs_v[mine, 0:STRIDE] = jnp.sum(grad_pooled[:, None, :] * keys3, axis=0).astype(bf16)
    gs_v[mine, STRIDE:KERNEL] = jnp.sum(grad_pooled[:, None, :] * upper3, axis=0).astype(bf16)
    gs_v[mine, KERNEL:] = stacked(*split3(sums[nb : nb + rc])[0:2])
    last = nb + rc
    kl_sum = (sums[last + 2 : last + 3] + sums[last + 1 : last + 2]) + sums[last : last + 1]
    loss_ref[...] = kl_sum * (1.0 / (rows * n))

    def gs_copy(dst):
        piece = gs_v.at[mine]
        return remote(piece, piece, all_sem.at[4], all_sem.at[5], 2 * dst + core)

    other_chips(lambda chip: gs_copy(chip).start())

    @pl.when(me < n - 1)
    def _():
        carry_copy(me + 1).start()

    @pl.when(me > 0)
    def _():
        carry_copy(me).wait_recv()

    before = jnp.concatenate([carry_v[7:8, :], grad_pooled[: nb - 1]], axis=0)
    grad_keys = grad_pooled[:, None, :] * gain_lo[None] + before[:, None, :] * gain_hi[None]
    gk_ref[...] = grad_keys.reshape(nb * STRIDE, DH).astype(bf16)

    wait_bytes(pool_v.at[pl.ds(0, half - 1), 0], all_sem.at[0])
    relay_copy(core).wait_send()
    wait_bytes(edge_v.at[pl.ds(0, half - 1), 0, pl.ds(0, 2)], all_sem.at[6])
    relay_edges(core).wait_send()
    wait_bytes(rs_v.at[pl.ds(0, half - 1)], all_sem.at[2])

    def drop_pair(c, _):
        pair_copy(c).wait_send()
        return 0

    lax.fori_loop(0, chunks, drop_pair, 0)
    side_copy().wait_send()

    @pl.when(me > 0)
    def _():
        halo_copy(me - 1).wait_send()

    @pl.when(me < n - 1)
    def _():
        carry_copy(me + 1).wait_send()

    wait_bytes(gs_v.at[pl.ds(0, half - 1)], all_sem.at[5])
    gf_v[core, 0:KERNEL] = loop(
        half - 1,
        lambda d, total: total + gs_v[d + 1, 0:KERNEL].astype(f32),
        gs_v[0, 0:KERNEL].astype(f32),
    )
    for d in range(half):
        if (d + 1) * rc <= hr:
            piece = gs_v[d, KERNEL:].astype(f32)
            gf_v[core, KERNEL + d * rc : KERNEL + (d + 1) * rc] = piece[0:rc] + piece[rc : 2 * rc]

    def gf_copy(slot):
        return remote(gf_v.at[slot], gf_v.at[slot], side_sem.at[6], side_sem.at[7], twin)

    gf_copy(core).start()
    wait_bytes(gs_v.at[pl.ds(0, half - 1)], all_sem.at[4])
    gf_copy(1 - core).wait_recv()
    ggain_ref[...] = gf_v[0, 0:KERNEL] + gf_v[1, 0:KERNEL]
    gcomp_ref[0:hr, :] = gf_v[0, KERNEL : KERNEL + hr]
    gcomp_ref[hr:DH, :] = gf_v[1, KERNEL : KERNEL + hr]
    gf_copy(core).wait_send()


def finish(*refs):
    sources, targets, sem = refs[:5], refs[5:10], refs[10]
    copies = [
        pltpu.make_async_copy(source, target, sem.at[i])
        for i, (source, target) in enumerate(zip(sources, targets))
    ]
    for copy in copies:
        copy.start()
    for copy in copies:
        copy.wait()


def body(n, keys, queries, teacher_map, slab_index, pos_gain, w_comp):
    rows, count = teacher_map.shape
    nb = count // n
    half = n // 2
    gb = rows if count <= 1024 else min(rows, LANES)
    rc = -(-(DH // 2) // half)
    slot_rows = nb - (-(rc + 1) // 8) * 8
    dma = pltpu.SemaphoreType.DMA
    vmem = pl.BlockSpec(memory_space=pltpu.VMEM)
    hbm = pl.BlockSpec(memory_space=pltpu.HBM)
    shapes = (
            jax.ShapeDtypeStruct((1, DH), f32),
            jax.ShapeDtypeStruct((rows, HEADS * DH), bf16),
            jax.ShapeDtypeStruct(keys.shape, bf16),
            jax.ShapeDtypeStruct((DH, DH), f32),
            jax.ShapeDtypeStruct((KERNEL, DH), f32),
        )
    results = pl.pallas_call(
        functools.partial(kernel, n, gb, rc),
        out_shape=shapes,
        in_specs=[pl.BlockSpec(memory_space=pltpu.SMEM)] + [hbm] * 5,
        out_specs=(vmem,) * 5,
        scratch_shapes=[
            pltpu.VMEM(keys.shape, bf16),
            pltpu.VMEM(pos_gain.shape, f32),
            pltpu.VMEM(w_comp.shape, bf16),
            pltpu.VMEM((rows, HEADS * DH), bf16),
            pltpu.VMEM((rows, count), bf16),
            pltpu.VMEM((half, 2, nb, DH), bf16),
            pltpu.VMEM((half, 2, 8, DH), f32),
            pltpu.VMEM((STRIDE, DH), bf16),
            pltpu.VMEM((count, DH), bf16),
            pltpu.VMEM((count, DH), bf16),
            pltpu.VMEM((DH, count), bf16),
            pltpu.VMEM((count, gb), f32),
            pltpu.VMEM((count, gb), f32),
            pltpu.VMEM((HEADS, count, gb), f32),
            pltpu.VMEM((HEADS, count, gb) if gb == rows else (8, LANES), f32),
            pltpu.VMEM((count, HEADS * gb), bf16),
            pltpu.VMEM((HEADS * gb, DH), bf16),
            pltpu.VMEM((count, gb), f32),
            pltpu.VMEM((count, gb), f32),
            pltpu.VMEM((HEADS, 8, gb), f32),
            pltpu.VMEM((HEADS, 8, gb), f32),
            pltpu.VMEM((2, half, slot_rows, DH), f32),
            pltpu.VMEM((half, slot_rows, DH), f32),
            pltpu.VMEM((half, nb - (-(rc + 3) // 16) * 16, DH), bf16),
            pltpu.VMEM((half, nb - (-(rc + 3) // 16) * 16, DH), bf16),
            pltpu.VMEM((half, KERNEL - (-2 * rc // 16) * 16, DH), bf16),
            pltpu.VMEM((2, KERNEL + DH // 2, DH), f32),
            pltpu.VMEM((nb, DH), f32),
            pltpu.VMEM((8, DH), f32),
            dma((6,)),
        ]
        + [dma((count // LANES,))] * 2
        + [dma((10,)), dma((10,))],
        compiler_params=pltpu.CompilerParams(
            collective_id=0, has_side_effects=True, vmem_limit_bytes=(24 if gb == rows else 56) * 1024 * 1024
        ),
    )(slab_index, *[pltpu.with_memory_space_constraint(x, pltpu.HBM) for x in (keys, pos_gain, w_comp, queries, teacher_map)])
    any_space = pl.BlockSpec(memory_space=pl.ANY)
    loss, gq, gk, gcomp, ggain = pl.pallas_call(
        finish,
        out_shape=shapes,
        in_specs=[any_space] * 5,
        out_specs=[any_space] * 5,
        scratch_shapes=[dma((5,))],
        compiler_params=pltpu.CompilerParams(vmem_limit_bytes=4 * 1024 * 1024),
    )(*results)
    return (loss[0, 0:1], gq, gk, gcomp, ggain)


def solution(mesh):
    in_specs = (
        P(("groups", "ctx"), None),
        P(("groups", "ctx"), None),
        P(("groups", "ctx"), None),
        P(("groups", "ctx")),
        P(),
        P(),
    )
    out_specs = (
        P("groups"),
        P(("groups", "ctx"), None),
        P(("groups", "ctx"), None),
        P("groups", None),
        P("groups", None),
    )
    return jax.shard_map(
        functools.partial(body, mesh.shape["ctx"]),
        mesh=mesh, in_specs=in_specs, out_specs=out_specs, check_vma=False,
    )
```

```python
import functools

import jax
import jax.numpy as jnp
from jax import lax
from jax.experimental import pallas as pl
from jax.experimental.pallas import tpu as pltpu
from jax.sharding import PartitionSpec as P

DH = 128
HEADS = 8
KERNEL = 32
STRIDE = 16
LANES = 128
TILE = 16
TILE_UNROLL = 8
HEAD_UNROLL = 8
GQ_UNROLL = 4
CHUNK_UNROLL = 4

big_negative = -1e30
loss_scale = 256.0
f32 = jnp.float32
bf16 = jnp.bfloat16


def split3(x):
    first = x.astype(bf16)
    rest = x - first.astype(f32)
    second = rest.astype(bf16)
    third = (rest - second.astype(f32)).astype(bf16)
    return first, second, third


def stacked(*pieces):
    fill = -sum(piece.shape[0] for piece in pieces) % 16
    if fill:
        pieces += (jnp.zeros((fill, DH), bf16),)
    return jnp.concatenate(pieces, axis=0)


def remote(src, dst, send_sem, recv_sem, device):
    return pltpu.make_async_remote_copy(
        src_ref=src,
        dst_ref=dst,
        send_sem=send_sem,
        recv_sem=recv_sem,
        device_id={"ctx": device},
        device_id_type=pl.DeviceIdType.MESH,
    )


def loop(count, step, start):
    if count <= 8:
        for i in range(count):
            start = step(i, start)
        return start
    return lax.fori_loop(0, count, step, start)


def aligned(i, size):
    return pl.ds(pl.multiple_of(i * size, size), size)


def fold(x, op):
    rows, lanes = x.shape
    return op(x.reshape(rows // 8, 8, lanes), axis=0)


def kernel(
    n, gb, rc,
    slab_ref, keys_hbm, gain_hbm, w_hbm, q_hbm, t_hbm,
    loss_ref, gq_ref, gk_ref, gcomp_ref, ggain_ref,
    keys_ref, gain_ref, w_ref, q_v, t_v, pool_v, edge_v, halo_v, pooled_v, comp_v, compt_v,
    bias_v, tp_v, s_v, u_v, g_v, qs_v, pk_v, wt_v, lse_v, cv_v, p_v, pair_v, rb_v, rs_v,
    gs_v, gf_v, gp_v, carry_v,
    local_sem, pair_s, pair_r, all_sem, side_sem,
):
    me = lax.axis_index("ctx")
    rows, count = t_v.shape
    nb = count // n
    inv = DH ** (-0.5)
    core = lax.rem(me, 2)
    mine = lax.div(me, 2)
    half = n // 2
    twin = me + 1 - 2 * core
    upper = lax.div(mine, half // 2)
    far = (half - 1) * (1 - upper)
    toward = 2 * upper - 1

    def other_chips(act):
        def step(i, _):
            chip = far + toward * i

            @pl.when(chip != mine)
            def _():
                act(chip)

            return 0

        lax.fori_loop(0, half, step, 0)

    barrier = pltpu.get_barrier_semaphore()

    def signal(device):
        pl.semaphore_signal(
            barrier, inc=1, device_id={"ctx": device}, device_id_type=pl.DeviceIdType.MESH
        )

    other_chips(lambda chip: signal(2 * chip + core))
    signal(twin)
    beyond = me - 1 + 2 * core
    inside = (beyond >= 0) & (beyond < n)

    @pl.when(inside)
    def _():
        signal(beyond)

    q_copy = pltpu.make_async_copy(q_hbm, q_v, local_sem.at[0])
    t_copy = pltpu.make_async_copy(t_hbm, t_v, local_sem.at[1])
    keys_copy = pltpu.make_async_copy(keys_hbm, keys_ref, local_sem.at[3])
    gain_copy = pltpu.make_async_copy(gain_hbm, gain_ref, local_sem.at[4])
    w_copy = pltpu.make_async_copy(w_hbm, w_ref, local_sem.at[5])
    keys_copy.start()
    gain_copy.start()
    t_copy.start()
    w_copy.start()
    q_copy.start()

    keys_copy.wait()
    gain_copy.wait()
    keys3 = keys_ref[...].astype(f32).reshape(nb, STRIDE, DH)
    gain_lo = gain_ref[0:STRIDE, :]
    gain_hi = gain_ref[STRIDE:KERNEL, :]
    low = jnp.sum(keys3 * gain_lo[None], axis=1)
    high = jnp.sum(keys3 * gain_hi[None], axis=1)
    pool_v[mine, core] = (low + jnp.concatenate([high[1:], high[:1]], axis=0)).astype(bf16)
    edge_v[mine, core, 0:1] = low[nb - 1 : nb]
    edge_v[mine, core, 1:2] = high[0:1]

    @pl.when(me == n - 1)
    def _():
        halo_v[...] = jnp.zeros((STRIDE, DH), bf16)

    @pl.when(me == 0)
    def _():
        carry_v[...] = jnp.zeros((8, DH), f32)

    place0 = slab_ref[0] * rows

    def prepare(base):
        def first(c, total):
            for l0 in range(0, gb, LANES):
                teach = t_v[pl.ds(base + l0, LANES), aligned(c, LANES)].astype(f32).T
                end = STRIDE * (c * LANES + lax.broadcasted_iota(jnp.int32, (LANES, LANES), 0)) + (KERNEL - 1)
                place = place0 + base + l0 + lax.broadcasted_iota(jnp.int32, (LANES, LANES), 1)
                visible = end <= place
                seen = jnp.where(visible, teach, 0.0)
                bias_v[aligned(c, LANES), l0 : l0 + LANES] = jnp.where(visible, 0.0, big_negative)
                tp_v[aligned(c, LANES), l0 : l0 + LANES] = seen
                part = fold(seen, jnp.sum)
                total = total[:l0 // LANES] + (total[l0 // LANES] + part,) + total[l0 // LANES + 1 :]
            return total

        zero = jnp.zeros((8, LANES), f32)
        total8 = loop(count // LANES, first, (zero,) * (gb // LANES))
        kl8 = zero
        for l0 in range(0, gb, LANES):
            total = jnp.sum(total8[l0 // LANES], axis=0, keepdims=True)
            safe = jnp.where(total > 0, total, 1.0)
            shift = 3.0 - jnp.log2(safe)

            def second(c, acc):
                at = (aligned(c, LANES), slice(l0, l0 + LANES))
                seen = tp_v[at]
                tprob = seen / safe
                tp_v[at] = tprob
                return acc + fold(tprob * (jnp.log2(jnp.maximum(seen, 1e-30)) + shift), jnp.sum)

            kl8 = loop(count // LANES, second, kl8)
        return kl8

    def stack(base):
        for h in range(HEADS):
            qs_v[h * gb : (h + 1) * gb, :] = q_v[pl.ds(base, gb), h * DH : (h + 1) * DH]

    whole = gb == rows
    e_v = u_v if whole else s_v
    pl.semaphore_wait(barrier, half + jnp.where(inside, 1, 0))


    def pool_copy(chip):
        block = pool_v.at[mine, core]
        return remote(block, block, all_sem.at[0], all_sem.at[1], 2 * chip + core)

    def edge_copy(chip):
        ends = edge_v.at[mine, core, pl.ds(0, 2)]
        return remote(ends, ends, all_sem.at[6], all_sem.at[7], 2 * chip + core)

    def relay_copy(c):
        blocks = pool_v.at[:, c]
        return remote(blocks, blocks, side_sem.at[8], side_sem.at[9], twin)

    def relay_edges(c):
        ends = edge_v.at[:, c, pl.ds(0, 2)]
        return remote(ends, ends, all_sem.at[8], all_sem.at[9], twin)

    def wait_bytes(ref, sem):
        pltpu.make_async_copy(ref, ref, sem).wait()

    other_chips(lambda chip: pool_copy(chip).start())
    other_chips(lambda chip: edge_copy(chip).start())

    def halo_copy(dst):
        return remote(
            keys_ref.at[pl.ds(0, STRIDE)], halo_v, side_sem.at[0], side_sem.at[1], dst
        )

    @pl.when(me > 0)
    def _():
        halo_copy(me - 1).start()

    t_copy.wait()
    kl_start = prepare(0) if whole else jnp.zeros((8, LANES), f32)
    w_copy.wait()
    q_copy.wait()
    if whole:
        stack(0)
    wait_bytes(pool_v.at[pl.ds(0, half - 1), 0], all_sem.at[1])
    relay_copy(core).start()
    wait_bytes(edge_v.at[pl.ds(0, half - 1), 0, pl.ds(0, 2)], all_sem.at[7])
    relay_edges(core).start()
    relay_copy(1 - core).wait_recv()
    relay_edges(1 - core).wait_recv()
    blocks = pool_v[...].reshape(n, nb, DH)
    last_row = lax.broadcasted_iota(jnp.int32, (n, nb, DH), 1) == nb - 1
    ends = edge_v[...].reshape(n, 8, DH)
    edges = ends[:, 0:1] + jnp.concatenate(
        [ends[1:, 1:2], jnp.zeros((1, 1, DH), f32)], axis=0
    )
    pooled = jnp.where(last_row, edges, blocks.astype(f32)).astype(bf16)
    pooled_v[...] = pooled.reshape(count, DH)
    comp_v[...] = jnp.dot(
        pooled_v[...], w_ref[...], preferred_element_type=f32
    ).astype(bf16)

    nt = (((1,), (1,)), ((), ()))
    tn = (((0,), (0,)), ((), ()))
    to_log2 = inv * 1.4426950408889634

    def probabilities(base, kl8):
        queries_at = pl.ds(base, gb)

        def head(h, _):
            qh = q_v[queries_at, aligned(h, DH)]

            def scores(c, top):
                s = lax.dot_general(
                    comp_v[aligned(c, LANES), :], qh, nt, preferred_element_type=f32
                )
                s = s * to_log2 + bias_v[aligned(c, LANES), :]
                s_v[h, aligned(c, LANES), :] = s
                return jnp.maximum(top, fold(s, jnp.max))

            top8 = loop(count // LANES, scores, jnp.full((8, gb), 2 * big_negative, f32))
            top = jnp.max(top8, axis=0, keepdims=True)

            def sums(c, total):
                return total + fold(jnp.exp2(s_v[h, aligned(c, LANES), :] - top), jnp.sum)

            total8 = loop(count // LANES, sums, jnp.zeros((8, gb), f32))
            total = jnp.sum(total8, axis=0, keepdims=True)
            lse = jnp.where(top > 0.5 * big_negative, top + jnp.log2(total), 0.0)
            lse_v[h] = jnp.broadcast_to(lse, (8, gb))
            return 0

        lax.fori_loop(0, HEADS, head, 0, unroll=HEAD_UNROLL)

        for l0 in range(0, gb, LANES):
            lanes = slice(l0, l0 + LANES)
            lse = [lse_v[h, :, lanes][None] for h in range(HEADS)]

            def ratios(c, carry):
                kl8, cv = carry
                at = aligned(c, TILE)
                x = []
                for h in range(HEADS):
                    x.append((s_v[h, at, lanes].reshape(TILE // 8, 8, LANES) - lse[h]))
                tops = x
                while len(tops) > 1:
                    tops = [jnp.maximum(a, b) for a, b in zip(tops[::2], tops[1::2])]
                peak = tops[0]
                u = [jnp.exp2(a - peak) for a in x]
                mass = u
                while len(mass) > 1:
                    mass = [a + b for a, b in zip(mass[::2], mass[1::2])]
                mass = mass[0]
                tprob = tp_v[at, lanes].reshape(TILE // 8, 8, LANES)
                weight = tprob / mass
                kl8 = kl8 - jnp.sum(tprob * (peak + jnp.log2(mass)), axis=0)
                pk_v[at, lanes] = jnp.exp2(peak).reshape(TILE, LANES)
                wt_v[at, lanes] = (loss_scale * weight).reshape(TILE, LANES)
                for h in range(HEADS):
                    e_v[h, at, lanes] = u[h].reshape(TILE, LANES)
                cv = tuple(a + jnp.sum(b * weight, axis=0) for a, b in zip(cv, u))
                return kl8, cv

            zero = jnp.zeros((8, LANES), f32)
            kl8, cv = lax.fori_loop(
                0, count // TILE, ratios, (kl8, (zero,) * HEADS), unroll=TILE_UNROLL
            )
            for h in range(HEADS):
                total = loss_scale * jnp.sum(cv[h], axis=0, keepdims=True)
                cv_v[h, :, lanes] = jnp.broadcast_to(total, (8, LANES))
        return kl8

    def block_grads(base, i, first, comp_part):
        c = first_chunk + chunk_step * i
        at = aligned(c, LANES)
        peak = pk_v[at, :].reshape(LANES // 8, 8, gb)
        weight = wt_v[at, :].reshape(LANES // 8, 8, gb)
        for h in range(HEADS):
            u = e_v[h, at, :].reshape(LANES // 8, 8, gb)
            g = u * (peak * cv_v[h][None] - weight)
            g_v[at, h * gb : (h + 1) * gb] = g.reshape(LANES, gb).astype(bf16)
        acc = jnp.dot(g_v[at, :], qs_v[...], preferred_element_type=f32)
        acc = acc * inv
        for k in range(LANES // nb):
            where = (k % 2, c * (LANES // nb // 2) + k // 2)
            if first:
                p_v[where + (slice(0, nb),)] = acc[k * nb : (k + 1) * nb]
            else:
                p_v[where + (slice(0, nb),)] += acc[k * nb : (k + 1) * nb]
        pieces = split3(acc)
        block = pooled_v[aligned(c, LANES), :]
        add = lax.dot_general(
            jnp.concatenate([block] * 3, axis=0),
            jnp.concatenate(pieces[::-1], axis=0),
            tn,
            preferred_element_type=f32,
        )
        return c, comp_part + add

    def query_grads(base, h0, h1):
        def head(h, _):
            gq = jnp.dot(compt_v[...], g_v[:, aligned(h, gb)], preferred_element_type=f32) * inv
            gq_ref[pl.ds(base, gb), aligned(h, DH)] = gq.T.astype(bf16)
            return 0

        lax.fori_loop(h0, h1, head, 0, unroll=GQ_UNROLL)

    used = nb + rc + 1

    def pair_copy(c):
        at = (pl.ds(c * per_chunk, per_chunk), pl.ds(0, nb))
        return remote(
            p_v.at[(1 - core,) + at], pair_v.at[at], pair_s.at[c], pair_r.at[c], twin
        )

    def side_copy():
        at = (slice(None), pl.ds(nb, rc + 1))
        return remote(
            p_v.at[(1 - core,) + at], pair_v.at[at], side_sem.at[4], side_sem.at[5], twin
        )

    def rs_copy(dst):
        return remote(
            rb_v.at[dst], rs_v.at[mine], all_sem.at[2], all_sem.at[3], 2 * dst + core
        )

    chunks = count // LANES
    per_chunk = LANES // nb // 2
    first_chunk = (chunks - 1) * (1 - upper)
    chunk_step = toward

    no_part = jnp.zeros((DH, DH), f32)
    if whole:
        kl8 = probabilities(0, kl_start)

        def chunk(i, part):
            c, part = block_grads(0, i, True, part)
            pair_copy(c).start()
            return part

        comp_part = lax.fori_loop(0, chunks, chunk, no_part, unroll=CHUNK_UNROLL)
    else:
        compt_v[...] = comp_v[...].astype(f32).T.astype(bf16)
        p_v[...] = jnp.zeros_like(p_v)

        def group(i, carry):
            kl8, part = carry
            base = pl.multiple_of(i * gb, gb)
            stack(base)
            kl8 = probabilities(base, kl8 + prepare(base))
            part = lax.fori_loop(0, chunks, lambda k, a: block_grads(base, k, False, a)[1], part)
            query_grads(base, 0, HEADS)
            return kl8, part

        kl8, comp_part = lax.fori_loop(0, rows // gb, group, (kl_start, no_part))

        def send_pair(c, _):
            pair_copy(c).start()
            return 0

        lax.fori_loop(0, chunks, send_pair, 0)

    kl_total = jnp.sum(jnp.sum(kl8, axis=0, keepdims=True), axis=1, keepdims=True)
    kl_row = jnp.broadcast_to(kl_total * 0.6931471805599453, (1, DH))
    hr = DH // 2
    for c in range(2):
        for d in range(half):
            if (d + 1) * rc <= hr:
                p_v[c, d, nb : nb + rc] = comp_part[c * hr + d * rc : c * hr + (d + 1) * rc]
            else:
                p_v[c, d, nb : nb + rc] = jnp.zeros((rc, DH), f32)
            p_v[c, d, nb + rc : used] = kl_row

    side_copy().start()
    if whole:
        compt_v[...] = comp_v[...].astype(f32).T.astype(bf16)

    side_copy().wait_recv()

    def forward(i, _):
        c = first_chunk + chunk_step * i
        pair_copy(c).wait_recv()
        chips = pl.ds(c * per_chunk, per_chunk)
        total = p_v[core, chips, 0:used] + pair_v[chips, 0:used]
        rb_v[chips, 0:nb] = total[:, 0:nb].astype(bf16)
        for k in range(per_chunk):
            rb_v[c * per_chunk + k, nb:] = stacked(
                total[k, nb : nb + rc].astype(bf16), *split3(total[k, nb + rc :])
            )
        for k in range(per_chunk):
            chip = c * per_chunk + k

            @pl.when(chip != mine)
            def _():
                rs_copy(chip).start()

        return 0

    loop(chunks, forward, 0)
    rs_v[mine] = rb_v[mine]
    if whole:
        query_grads(0, 0, HEADS)

    @pl.when(me < n - 1)
    def _():
        halo_copy(me).wait_recv()

    upper3 = jnp.concatenate(
        [keys3[1:], halo_v[...].astype(f32).reshape(1, STRIDE, DH)], axis=0
    )

    wait_bytes(rs_v.at[pl.ds(0, half - 1)], all_sem.at[3])
    sums = loop(half - 1, lambda d, total: total + rs_v[d + 1].astype(f32), rs_v[0].astype(f32))
    own = sums[0:nb]
    own3 = split3(own)
    gp3 = lax.dot_general(
        jnp.concatenate(own3, axis=0), w_ref[...], nt, preferred_element_type=f32
    )
    grad_pooled = (gp3[2 * nb :] + gp3[nb : 2 * nb]) + gp3[:nb]
    gp_v[...] = grad_pooled

    def carry_copy(dst):
        return remote(
            gp_v.at[pl.ds(nb - 8, 8)], carry_v, side_sem.at[2], side_sem.at[3], dst
        )

    gs_v[mine, 0:STRIDE] = jnp.sum(grad_pooled[:, None, :] * keys3, axis=0).astype(bf16)
    gs_v[mine, STRIDE:KERNEL] = jnp.sum(grad_pooled[:, None, :] * upper3, axis=0).astype(bf16)
    gs_v[mine, KERNEL:] = stacked(*split3(sums[nb : nb + rc])[0:2])
    last = nb + rc
    kl_sum = (sums[last + 2 : last + 3] + sums[last + 1 : last + 2]) + sums[last : last + 1]
    loss_ref[...] = kl_sum * (1.0 / (rows * n))

    def gs_copy(dst):
        piece = gs_v.at[mine]
        return remote(piece, piece, all_sem.at[4], all_sem.at[5], 2 * dst + core)

    other_chips(lambda chip: gs_copy(chip).start())

    @pl.when(me < n - 1)
    def _():
        carry_copy(me + 1).start()

    @pl.when(me > 0)
    def _():
        carry_copy(me).wait_recv()

    before = jnp.concatenate([carry_v[7:8, :], grad_pooled[: nb - 1]], axis=0)
    grad_keys = grad_pooled[:, None, :] * gain_lo[None] + before[:, None, :] * gain_hi[None]
    gk_ref[...] = grad_keys.reshape(nb * STRIDE, DH).astype(bf16)

    wait_bytes(pool_v.at[pl.ds(0, half - 1), 0], all_sem.at[0])
    relay_copy(core).wait_send()
    wait_bytes(edge_v.at[pl.ds(0, half - 1), 0, pl.ds(0, 2)], all_sem.at[6])
    relay_edges(core).wait_send()
    wait_bytes(rs_v.at[pl.ds(0, half - 1)], all_sem.at[2])

    def drop_pair(c, _):
        pair_copy(c).wait_send()
        return 0

    lax.fori_loop(0, chunks, drop_pair, 0)
    side_copy().wait_send()

    @pl.when(me > 0)
    def _():
        halo_copy(me - 1).wait_send()

    @pl.when(me < n - 1)
    def _():
        carry_copy(me + 1).wait_send()

    wait_bytes(gs_v.at[pl.ds(0, half - 1)], all_sem.at[5])
    gf_v[core, 0:KERNEL] = loop(
        half - 1,
        lambda d, total: total + gs_v[d + 1, 0:KERNEL].astype(f32),
        gs_v[0, 0:KERNEL].astype(f32),
    )
    for d in range(half):
        if (d + 1) * rc <= hr:
            piece = gs_v[d, KERNEL:].astype(f32)
            gf_v[core, KERNEL + d * rc : KERNEL + (d + 1) * rc] = piece[0:rc] + piece[rc : 2 * rc]

    def gf_copy(slot):
        return remote(gf_v.at[slot], gf_v.at[slot], side_sem.at[6], side_sem.at[7], twin)

    gf_copy(core).start()
    wait_bytes(gs_v.at[pl.ds(0, half - 1)], all_sem.at[4])
    gf_copy(1 - core).wait_recv()
    ggain_ref[...] = gf_v[0, 0:KERNEL] + gf_v[1, 0:KERNEL]
    gcomp_ref[0:hr, :] = gf_v[0, KERNEL : KERNEL + hr]
    gcomp_ref[hr:DH, :] = gf_v[1, KERNEL : KERNEL + hr]
    gf_copy(core).wait_send()


def finish(*refs):
    sources, targets, sem = refs[:5], refs[5:10], refs[10]
    copies = [
        pltpu.make_async_copy(source, target, sem.at[i])
        for i, (source, target) in enumerate(zip(sources, targets))
    ]
    for copy in copies:
        copy.start()
    for copy in copies:
        copy.wait()


def body(n, keys, queries, teacher_map, slab_index, pos_gain, w_comp):
    rows, count = teacher_map.shape
    nb = count // n
    half = n // 2
    gb = rows if count <= 1024 else min(rows, LANES)
    rc = -(-(DH // 2) // half)
    slot_rows = nb - (-(rc + 1) // 8) * 8
    dma = pltpu.SemaphoreType.DMA
    vmem = pl.BlockSpec(memory_space=pltpu.VMEM)
    hbm = pl.BlockSpec(memory_space=pltpu.HBM)
    shapes = (
            jax.ShapeDtypeStruct((1, DH), f32),
            jax.ShapeDtypeStruct((rows, HEADS * DH), bf16),
            jax.ShapeDtypeStruct(keys.shape, bf16),
            jax.ShapeDtypeStruct((DH, DH), f32),
            jax.ShapeDtypeStruct((KERNEL, DH), f32),
        )
    results = pl.pallas_call(
        functools.partial(kernel, n, gb, rc),
        out_shape=shapes,
        in_specs=[pl.BlockSpec(memory_space=pltpu.SMEM)] + [hbm] * 5,
        out_specs=(vmem,) * 5,
        scratch_shapes=[
            pltpu.VMEM(keys.shape, bf16),
            pltpu.VMEM(pos_gain.shape, f32),
            pltpu.VMEM(w_comp.shape, bf16),
            pltpu.VMEM((rows, HEADS * DH), bf16),
            pltpu.VMEM((rows, count), bf16),
            pltpu.VMEM((half, 2, nb, DH), bf16),
            pltpu.VMEM((half, 2, 8, DH), f32),
            pltpu.VMEM((STRIDE, DH), bf16),
            pltpu.VMEM((count, DH), bf16),
            pltpu.VMEM((count, DH), bf16),
            pltpu.VMEM((DH, count), bf16),
            pltpu.VMEM((count, gb), f32),
            pltpu.VMEM((count, gb), f32),
            pltpu.VMEM((HEADS, count, gb), f32),
            pltpu.VMEM((HEADS, count, gb) if gb == rows else (8, LANES), f32),
            pltpu.VMEM((count, HEADS * gb), bf16),
            pltpu.VMEM((HEADS * gb, DH), bf16),
            pltpu.VMEM((count, gb), f32),
            pltpu.VMEM((count, gb), f32),
            pltpu.VMEM((HEADS, 8, gb), f32),
            pltpu.VMEM((HEADS, 8, gb), f32),
            pltpu.VMEM((2, half, slot_rows, DH), f32),
            pltpu.VMEM((half, slot_rows, DH), f32),
            pltpu.VMEM((half, nb - (-(rc + 3) // 16) * 16, DH), bf16),
            pltpu.VMEM((half, nb - (-(rc + 3) // 16) * 16, DH), bf16),
            pltpu.VMEM((half, KERNEL - (-2 * rc // 16) * 16, DH), bf16),
            pltpu.VMEM((2, KERNEL + DH // 2, DH), f32),
            pltpu.VMEM((nb, DH), f32),
            pltpu.VMEM((8, DH), f32),
            dma((6,)),
        ]
        + [dma((count // LANES,))] * 2
        + [dma((10,)), dma((10,))],
        compiler_params=pltpu.CompilerParams(
            collective_id=0, has_side_effects=True, vmem_limit_bytes=(24 if gb == rows else 56) * 1024 * 1024
        ),
    )(slab_index, *[pltpu.with_memory_space_constraint(x, pltpu.HBM) for x in (keys, pos_gain, w_comp, queries, teacher_map)])
    any_space = pl.BlockSpec(memory_space=pl.ANY)
    loss, gq, gk, gcomp, ggain = pl.pallas_call(
        finish,
        out_shape=shapes,
        in_specs=[any_space] * 5,
        out_specs=[any_space] * 5,
        scratch_shapes=[dma((5,))],
        compiler_params=pltpu.CompilerParams(vmem_limit_bytes=4 * 1024 * 1024),
    )(*results)
    return (loss[0, 0:1], gq, gk, gcomp, ggain)


def solution(mesh):
    in_specs = (
        P(("groups", "ctx"), None),
        P(("groups", "ctx"), None),
        P(("groups", "ctx"), None),
        P(("groups", "ctx")),
        P(),
        P(),
    )
    out_specs = (
        P("groups"),
        P(("groups", "ctx"), None),
        P(("groups", "ctx"), None),
        P("groups", None),
        P("groups", None),
    )
    return jax.shard_map(
        functools.partial(body, mesh.shape["ctx"]),
        mesh=mesh, in_specs=in_specs, out_specs=out_specs, check_vma=False,
    )
```
